32 devices in a mesh: shot: 2 (over core), gx: 4 (over y, x), gy: 4 (over z).
Axes of the slice: x: 2, y: 2, z: 4, core: 2. Of those that a mesh axis runs over, the one named last changes fastest.
Arguments:
- stress_fields: float32 [4, 3, 6, 64, 64, 128], P('shot', None, None, 'gx', 'gy'), may hold values from -6 to 6
- velocity_fields: float32 [4, 3, 3, 64, 64, 128], P('shot', None, None, 'gx', 'gy'), may hold values from -6 to 6
- lame: float32 [64, 64, 128], P('gx', 'gy'), may hold values from 0.4 to 1.6
- shear: float32 [64, 64, 128], P('gx', 'gy'), may hold values from 0.25 to 1
- density: float32 [64, 64, 128], P('gx', 'gy'), may hold values from 0.8 to 2
- lame_change: float32 [64, 64, 128], P('gx', 'gy'), may hold values from -3 to 3
- shear_change: float32 [64, 64, 128], P('gx', 'gy'), may hold values from -3 to 3
- density_change: float32 [64, 64, 128], P('gx', 'gy'), may hold values from -3 to 3
- source_cell: int32 [4], P('shot'), may hold values from 0 to 524287
- source_amp: float32 [4], P('shot'), may hold values from 4 to 16
- receiver_cell: int32 [4, 512], P('shot'), may hold values from 0 to 4095
Outputs:
- new_velocity: float32 [4, 2, 3, 64, 64, 128], P('shot', None, None, 'gx', 'gy')
- new_stress: float32 [4, 2, 6, 64, 64, 128], P('shot', None, None, 'gx', 'gy')
- kernels: float32 [3, 64, 64, 128], P(None, ('gx', 'shot'), 'gy')
The draws below stay inside these ranges and needn't reach their ends.
Inputs may be any that keep to these rules, and one draw needn't show every extreme that they name: source_cell[s] = x * 64 * 128 + y * 128 + z for the source's grid cell (x, y, z). receiver_cell[s, r] = x * 64 + y for a receiver at (x, y, 2); several receivers of a shot may share a cell.
All inputs are finite; a program needn't handle non-finite values.
Results may differ from the reference program's by a relative error of at most 0.0003.
Values sent between devices are 32-bit elements; how exact they have to be, the bound alone decides.
A program may use at most 128 MiB of HBM per device.

```python
import math
import jax
import jax.numpy as jnp
from jax import lax

NZ = 128
REC = 512
RDEPTH = 2
NX = 64
NY = 64
SHOTS = 4


def place_ends(values, own_key, low, high):
    longest = values.shape.index(max(values.shape))
    spots = []
    for shift in (0, 1):
        where = [jax.random.randint(jax.random.fold_in(own_key, axis), (), 0, length) for axis, length in enumerate(values.shape)]
        where[longest] = (where[longest] + shift) % values.shape[longest]
        spots.append(tuple(where))
    return values.at[spots[0]].set(low).at[spots[1]].set(high)


def level_of(rng, shape, split, smallest, high):
    level, own = 1.0, jax.random.fold_in(rng, 6)
    for position, blocks in split:
        heights = jnp.exp(jax.random.uniform(jax.random.fold_in(own, position), (blocks,), jnp.float32, smallest / len(split), high / len(split)))
        level = level * jnp.repeat(heights, shape[position] // blocks).reshape([-1 if axis == position else 1 for axis in range(len(shape))])
    return level


def normal_values(key, extent, spread, most, split=(), kind=jnp.bfloat16):
    level = level_of(key, extent, split, -0.22, 0.18) if split else 1.0
    values = jax.random.normal(key, extent, jnp.float32) * spread * level
    return jnp.minimum(jnp.maximum(values, -most), most).astype(kind)


def setup_inputs(seed: int = 0) -> dict:
    streams_of = jax.random.split(jax.random.key(seed), 12)
    return {
        "stress_fields": normal_values(streams_of[0], (SHOTS, 3, 6, NX, NY, NZ), 1.0, 6.0, ((0, 2), (3, 4), (4, 4)), jnp.float32),
        "velocity_fields": normal_values(streams_of[1], (SHOTS, 3, 3, NX, NY, NZ), 1.0, 6.0, ((0, 2), (3, 4), (4, 4)), jnp.float32),
        "lame": jnp.clip(jnp.exp(math.log(1.6) - 1.3862944 * jax.random.uniform(streams_of[2], (NX, NY, NZ), jnp.float32) ** level_of(streams_of[2], (NX, NY, NZ), ((0, 4), (1, 4)), -0.2, 0.2)), 0.4, 1.6),
        "shear": jnp.clip(jnp.exp(math.log(1.0) - 1.3862944 * jax.random.uniform(streams_of[3], (NX, NY, NZ), jnp.float32) ** level_of(streams_of[3], (NX, NY, NZ), ((0, 4), (1, 4)), -0.2, 0.2)), 0.25, 1.0),
        "density": jnp.clip(jnp.exp(math.log(2.0) - 0.9162907 * jax.random.uniform(streams_of[4], (NX, NY, NZ), jnp.float32) ** level_of(streams_of[4], (NX, NY, NZ), ((0, 4), (1, 4)), -0.2, 0.2)), 0.8, 2.0),
        "lame_change": normal_values(streams_of[5], (NX, NY, NZ), 0.5, 3.0, ((0, 4), (1, 4)), jnp.float32),
        "shear_change": normal_values(streams_of[6], (NX, NY, NZ), 0.5, 3.0, ((0, 4), (1, 4)), jnp.float32),
        "density_change": normal_values(streams_of[7], (NX, NY, NZ), 0.5, 3.0, ((0, 4), (1, 4)), jnp.float32),
        "source_cell": place_ends(jax.random.randint(streams_of[8], (SHOTS,), 0, NX * NY * NZ), jax.random.fold_in(streams_of[8], 1), 0, (NX * NY * NZ) - 1).astype(jnp.int32),
        "source_amp": jnp.clip(jnp.exp(math.log(16.0) - 1.3862944 * jax.random.uniform(streams_of[9], (SHOTS,), jnp.float32) ** level_of(streams_of[9], (SHOTS,), ((0, 2),), -0.2, 0.2)), 4.0, 16.0),
        "receiver_cell": place_ends(jax.random.randint(streams_of[10], (SHOTS, REC), 0, NX * NY), jax.random.fold_in(streams_of[10], 1), 0, (NX * NY) - 1).astype(jnp.int32),
    }


courant = 0.25
stress_upper_rows = (0,)
stress_lower_rows = (3, 4)
stress_upper_columns = (1,)
stress_lower_columns = (3, 5)
motion_upper_rows = (1, 2)
motion_lower_rows = (0,)
motion_upper_columns = (0, 2)
motion_lower_columns = (1,)


def forward_rows(quantity, upper_face):
    return jnp.concatenate([quantity[..., 1:, :, :], upper_face], axis=-3) - quantity


def backward_rows(quantity, lower_face):
    return quantity - jnp.concatenate([lower_face, quantity[..., :-1, :, :]], axis=-3)


def forward_columns(quantity, upper_face):
    return jnp.concatenate([quantity[..., 1:, :], upper_face], axis=-2) - quantity


def backward_columns(quantity, lower_face):
    return quantity - jnp.concatenate([lower_face, quantity[..., :-1, :]], axis=-2)


def forward_depth(quantity):
    return jnp.concatenate([quantity[..., 1:], jnp.zeros_like(quantity[..., :1])], axis=-1) - quantity


def backward_depth(quantity):
    return quantity - jnp.concatenate([jnp.zeros_like(quantity[..., :1]), quantity[..., :-1]], axis=-1)


def component(array, index):
    return array[..., index, :, :, :]


def wavefield(array, index):
    return array[..., index, :, :, :, :]


def accelerations(stress, upper_rows, lower_rows, upper_columns, lower_columns):
    accel_x = forward_rows(component(stress, 0), component(upper_rows, 0)) + backward_columns(component(stress, 3), component(lower_columns, 0)) + backward_depth(component(stress, 4))
    accel_y = backward_rows(component(stress, 3), component(lower_rows, 0)) + forward_columns(component(stress, 1), component(upper_columns, 0)) + backward_depth(component(stress, 5))
    accel_z = backward_rows(component(stress, 4), component(lower_rows, 1)) + backward_columns(component(stress, 5), component(lower_columns, 1)) + forward_depth(component(stress, 2))
    return jnp.stack([accel_x, accel_y, accel_z], axis=-4)


def strains(velocity, upper_rows, lower_rows, upper_columns, lower_columns):
    strain_xx = backward_rows(component(velocity, 0), component(lower_rows, 0))
    strain_yy = backward_columns(component(velocity, 1), component(lower_columns, 0))
    strain_zz = backward_depth(component(velocity, 2))
    shear_xy = forward_columns(component(velocity, 0), component(upper_columns, 0)) + forward_rows(component(velocity, 1), component(upper_rows, 0))
    shear_xz = forward_depth(component(velocity, 0)) + forward_rows(component(velocity, 2), component(upper_rows, 1))
    shear_yz = forward_depth(component(velocity, 1)) + forward_columns(component(velocity, 2), component(upper_columns, 1))
    return jnp.stack([strain_xx, strain_yy, strain_zz, shear_xy, shear_xz, shear_yz], axis=-4)


def moduli(strain, first, second):
    trace = component(strain, 0) + component(strain, 1) + component(strain, 2)
    parts = [first * trace + 2.0 * second * component(strain, index) for index in range(3)]
    parts = parts + [second * component(strain, index) for index in range(3, 6)]
    return jnp.stack(parts, axis=-4)


def update_velocity(velocity, accel, buoyancy, density_change, source_field, record_field):
    scaled = courant * buoyancy
    base = wavefield(velocity, 0) + scaled * wavefield(accel, 0)
    base = base.at[..., 2, :, :, :].add(scaled * source_field)
    born = wavefield(velocity, 1) + scaled * (wavefield(accel, 1) - density_change * buoyancy * wavefield(accel, 0))
    adjoint = wavefield(velocity, 2) + scaled * wavefield(accel, 2)
    adjoint = adjoint.at[..., 2, :, :, :].add(scaled * record_field * component(born, 2))
    return jnp.stack([base, born, adjoint], axis=-5)


def update_stress(stress, strain, lame, shear, lame_change, shear_change):
    born = wavefield(stress, 1) + courant * (moduli(wavefield(strain, 1), lame, shear) + moduli(wavefield(strain, 0), lame_change, shear_change))
    adjoint = wavefield(stress, 2) + courant * moduli(wavefield(strain, 2), lame, shear)
    return jnp.stack([born, adjoint], axis=-5)


def kernel_terms(strain, new_stress, accel, velocity_next, buoyancy):
    base_strain = wavefield(strain, 0)
    adjoint_stress = wavefield(new_stress, 1)
    trace_product = (component(base_strain, 0) + component(base_strain, 1) + component(base_strain, 2)) * (component(adjoint_stress, 0) + component(adjoint_stress, 1) + component(adjoint_stress, 2))
    shear_sum = 2.0 * (component(base_strain, 0) * component(adjoint_stress, 0) + component(base_strain, 1) * component(adjoint_stress, 1) + component(base_strain, 2) * component(adjoint_stress, 2))
    shear_sum = shear_sum + component(base_strain, 3) * component(adjoint_stress, 3) + component(base_strain, 4) * component(adjoint_stress, 4) + component(base_strain, 5) * component(adjoint_stress, 5)
    density_sum = buoyancy * jnp.sum(wavefield(accel, 0) * wavefield(velocity_next, 2), axis=-4)
    return jnp.stack([trace_product, shear_sum, density_sum], axis=-4)


def zero_faces(fields, upper_rows, lower_rows, upper_columns, lower_columns):
    leading = fields.shape[:-4]
    rows, cols, depth = fields.shape[-3:]
    return (jnp.zeros(leading + (len(upper_rows), 1, cols, depth), fields.dtype),
            jnp.zeros(leading + (len(lower_rows), 1, cols, depth), fields.dtype),
            jnp.zeros(leading + (len(upper_columns), rows, 1, depth), fields.dtype),
            jnp.zeros(leading + (len(lower_columns), rows, 1, depth), fields.dtype))


def reference(stress_fields, velocity_fields, lame, shear, density, lame_change, shear_change, density_change, source_cell, source_amp, receiver_cell):
    rows, cols, depth = lame.shape
    real_type = lame.dtype
    buoyancy = 1.0 / density
    row_ids = jnp.arange(rows, dtype=jnp.int32)
    column_ids = jnp.arange(cols, dtype=jnp.int32)
    depth_ids = jnp.arange(depth, dtype=jnp.int32)
    plane = (depth_ids == RDEPTH).astype(real_type)

    def one_shot(total, inputs):
        stress, velocity, cell, amplitude, receivers = inputs
        source_row = cell // (cols * depth)
        source_column = (cell // depth) % cols
        source_level = cell % depth
        source_field = amplitude * (row_ids == source_row).astype(real_type)[:, None, None] * (column_ids == source_column).astype(real_type)[None, :, None] * (depth_ids == source_level).astype(real_type)[None, None, :]
        receiver_rows = receivers // cols
        receiver_columns = receivers % cols
        row_marks = (receiver_rows[:, None] == row_ids[None, :]).astype(real_type)
        column_marks = (receiver_columns[:, None] == column_ids[None, :]).astype(real_type)
        counts = jnp.dot(row_marks.T, column_marks, precision=lax.Precision.HIGHEST, preferred_element_type=jnp.float32)
        record_field = counts[:, :, None] * plane
        accel = accelerations(stress, *zero_faces(stress, stress_upper_rows, stress_lower_rows, stress_upper_columns, stress_lower_columns))
        velocity_next = update_velocity(velocity, accel, buoyancy, density_change, source_field, record_field)
        strain = strains(velocity_next, *zero_faces(velocity_next, motion_upper_rows, motion_lower_rows, motion_upper_columns, motion_lower_columns))
        new_stress = update_stress(stress, strain, lame, shear, lame_change, shear_change)
        terms = kernel_terms(strain, new_stress, accel, velocity_next, buoyancy)
        return total + terms, (velocity_next[1:], new_stress)

    start = jnp.zeros((3, rows, cols, depth), jnp.float32)
    total, outputs = lax.scan(one_shot, start, (stress_fields, velocity_fields, source_cell, source_amp, receiver_cell))
    return outputs[0], outputs[1], total / SHOTS
```

```python
import functools

import jax
import jax.numpy as jnp
from jax import lax
from jax.experimental import pallas as pl
from jax.experimental.pallas import tpu as pltpu
from jax.sharding import PartitionSpec as P

RDEPTH = 2
COURANT = 0.25
MESH = pl.DeviceIdType.MESH


def shifted_up(tile, halo, axis):
    length = tile.shape[axis]
    index = lax.broadcasted_iota(jnp.int32, tile.shape, axis)
    return jnp.where(index == length - 1, halo, pltpu.roll(tile, length - 1, axis))


def shifted_down(tile, halo, axis):
    index = lax.broadcasted_iota(jnp.int32, tile.shape, axis)
    return jnp.where(index == 0, halo, pltpu.roll(tile, 1, axis))


def motion_kernel(
    every_column,
    stress,
    velocity,
    density,
    density_change,
    source_cell,
    source_amp,
    receivers,
    motion_out,
    density_term,
    up_rows,
    low_rows,
    up_cols,
    low_cols,
    st,
    mo,
    record,
    st_up_rows,
    st_low_rows,
    st_up_cols,
    st_low_cols,
    st_up_cols_out,
    st_low_cols_out,
    up_cols_out,
    low_cols_out,
    load_sem,
    store_sem,
    send_sem,
    recv_sem,
):
    shots, waves, _, rows, cols, depth = stress.shape
    gx, gy = lax.axis_index("gx"), lax.axis_index("gy")
    nx, ny = lax.axis_size("gx"), lax.axis_size("gy")
    has_low_x, has_up_x = gx > 0, gx < nx - 1
    has_low_y, has_up_y = gy > 0, gy < ny - 1
    sides = (
        (has_low_x, {"gx": gx - 1}),
        (has_up_x, {"gx": gx + 1}),
        (has_low_y, {"gy": gy - 1}),
        (has_up_y, {"gy": gy + 1}),
    )
    barrier = pltpu.get_barrier_semaphore()
    for present, device in sides:

        @pl.when(present)
        def _(device=device):
            pl.semaphore_signal(barrier, inc=1, device_id=device, device_id_type=MESH)

    loads = []
    for s in range(shots):
        for which, (src, dst) in enumerate(((stress, st), (velocity, mo))):
            copy = pltpu.make_async_copy(src.at[s], dst.at[s], load_sem.at[s, which])
            copy.start()
            loads.append(copy)

    def face(src, dst, slot, device):
        return pltpu.make_async_remote_copy(
            src_ref=src,
            dst_ref=dst,
            send_sem=send_sem.at[slot],
            recv_sem=recv_sem.at[slot],
            device_id=device,
            device_id_type=MESH,
        )

    low_x, up_x, low_y, up_y = (device for _, device in sides)
    stress_rows = (
        (face(stress.at[:, :, 0, 0], st_up_rows, 0, low_x), has_low_x, has_up_x, st_up_rows),
        (
            face(stress.at[:, :, pl.ds(3, 2), rows - 1], st_low_rows, 1, up_x),
            has_up_x,
            has_low_x,
            st_low_rows,
        ),
    )
    stress_cols = [
        (
            (
                face(st_up_cols_out.at[s], st_up_cols.at[s], 2 + 2 * s, low_y),
                has_low_y,
                has_up_y,
                st_up_cols.at[s],
            ),
            (
                face(st_low_cols_out.at[s], st_low_cols.at[s], 3 + 2 * s, up_y),
                has_up_y,
                has_low_y,
                st_low_cols.at[s],
            ),
        )
        for s in range(shots)
    ]
    base = 2 + 2 * shots
    motion_faces = [
        (
            (
                face(mo.at[s, :, pl.ds(1, 2), 0], up_rows.at[s], base + 4 * s, low_x),
                has_low_x,
                has_up_x,
                up_rows.at[s],
            ),
            (
                face(mo.at[s, :, 0, rows - 1], low_rows.at[s], base + 4 * s + 1, up_x),
                has_up_x,
                has_low_x,
                low_rows.at[s],
            ),
            (
                face(up_cols_out.at[s], up_cols.at[s], base + 4 * s + 2, low_y),
                has_low_y,
                has_up_y,
                up_cols.at[s],
            ),
            (
                face(low_cols_out.at[s], low_cols.at[s], base + 4 * s + 3, up_y),
                has_up_y,
                has_low_y,
                low_cols.at[s],
            ),
        )
        for s in range(shots)
    ]

    def send(faces):
        for copy, sends, _, _ in faces:

            @pl.when(sends)
            def _(copy=copy):
                copy.start()

    def receive(faces):
        for copy, _, receives, landing in faces:

            @pl.when(receives)
            def _(copy=copy):
                copy.wait_recv()

            @pl.when(jnp.logical_not(receives))
            def _(landing=landing):
                landing[...] = jnp.zeros(landing.shape, jnp.float32)

    def sent(faces):
        for copy, sends, _, _ in faces:

            @pl.when(sends)
            def _(copy=copy):
                copy.wait_send()

    neighbours = (
        has_low_x.astype(jnp.int32)
        + has_up_x.astype(jnp.int32)
        + has_low_y.astype(jnp.int32)
        + has_up_y.astype(jnp.int32)
    )
    pl.semaphore_wait(barrier, neighbours)
    send(stress_rows)
    row_start, col_start = gx * rows, gy * cols

    for s in range(shots):
        loads[2 * s].wait()
        for w in range(waves):
            st_up_cols_out[s, w] = st[s, w, 1, :, 0, :]
            st_low_cols_out[s, w, 0] = st[s, w, 3, :, cols - 1, :]
            st_low_cols_out[s, w, 1] = st[s, w, 5, :, cols - 1, :]
        send(stress_cols[s])

    count = receivers.shape[1]
    plane = (lax.broadcasted_iota(jnp.int32, (count, depth), 1) == RDEPTH).astype(jnp.bfloat16)
    local = lax.broadcasted_iota(jnp.int32, (rows, cols, count), 0) + row_start
    cell = local * every_column + (
        lax.broadcasted_iota(jnp.int32, (rows, cols, count), 1) + col_start
    )
    cell = cell.reshape(rows * cols, count)
    for s in range(shots):
        marks = jnp.where(receivers[pl.ds(s, 1), :] == cell, 1.0, 0.0).astype(jnp.bfloat16)
        field = jnp.dot(marks, plane, preferred_element_type=jnp.float32)
        record[s] = field.reshape(rows, cols, depth)

    place = (
        lax.broadcasted_iota(jnp.int32, (cols, depth), 0) + col_start
    ) * depth + lax.broadcasted_iota(jnp.int32, (cols, depth), 1)
    receive(stress_rows)
    stores = []
    for s in range(shots):
        loads[2 * s + 1].wait()
        receive(stress_cols[s])
        target, amplitude = source_cell[s], source_amp[s]

        def row(x, carry, s=s, target=target, amplitude=amplitude):
            after = lax.rem(x + 1, rows)
            before = lax.rem(x + rows - 1, rows)
            last, first = x == rows - 1, x == 0
            buoyancy = 1.0 / density[x]
            scaled = COURANT * buoyancy
            change = density_change[x] * buoyancy
            accel = []
            for w in range(waves):
                sxx, syy, szz = st[s, w, 0, x], st[s, w, 1, x], st[s, w, 2, x]
                sxy, sxz, syz = st[s, w, 3, x], st[s, w, 4, x], st[s, w, 5, x]
                sxx_after = jnp.where(last, st_up_rows[s, w], st[s, w, 0, after])
                sxy_before = jnp.where(first, st_low_rows[s, w, 0], st[s, w, 3, before])
                sxz_before = jnp.where(first, st_low_rows[s, w, 1], st[s, w, 4, before])
                syy_halo = st_up_cols[s, w, pl.ds(x, 1), :]
                sxy_halo = st_low_cols[s, w, 0, pl.ds(x, 1), :]
                syz_halo = st_low_cols[s, w, 1, pl.ds(x, 1), :]
                accel.append(
                    (
                        (sxx_after - sxx)
                        + (sxy - shifted_down(sxy, sxy_halo, 0))
                        + (sxz - shifted_down(sxz, 0.0, 1)),
                        (sxy - sxy_before)
                        + (shifted_up(syy, syy_halo, 0) - syy)
                        + (syz - shifted_down(syz, 0.0, 1)),
                        (sxz - sxz_before)
                        + (syz - shifted_down(syz, syz_halo, 0))
                        + (shifted_up(szz, 0.0, 1) - szz),
                    )
                )
            here = place + (x + row_start) * (every_column * depth)
            source = jnp.where(here == target, amplitude, 0.0)
            marks = record[s, x]
            total = None
            for c in range(3):
                first_wave = mo[s, 0, c, x] + scaled * accel[0][c]
                born = mo[s, 1, c, x] + scaled * (accel[1][c] - change * accel[0][c])
                adjoint = mo[s, 2, c, x] + scaled * accel[2][c]
                if c == 2:
                    first_wave = first_wave + scaled * source
                    adjoint = adjoint + scaled * marks * born
                mo[s, 0, c, x] = first_wave
                mo[s, 1, c, x] = born
                mo[s, 2, c, x] = adjoint
                term = accel[0][c] * adjoint
                total = term if total is None else total + term
            total = buoyancy * total
            if s == 0:
                density_term[x] = total
            else:
                density_term[x] = density_term[x] + total
            return carry

        lax.fori_loop(0, rows, row, 0)
        for w in range(waves):
            up_cols_out[s, w, 0] = mo[s, w, 0, :, 0, :]
            up_cols_out[s, w, 1] = mo[s, w, 2, :, 0, :]
            low_cols_out[s, w] = mo[s, w, 1, :, cols - 1, :]
        send(motion_faces[s])
        copy = pltpu.make_async_copy(mo.at[s], motion_out.at[s], store_sem.at[s])
        copy.start()
        stores.append(copy)
    for s in range(shots):
        receive(motion_faces[s])
    sent(stress_rows)
    for s in range(shots):
        sent(stress_cols[s])
        sent(motion_faces[s])
        stores[s].wait()


def stress_kernel(
    stress,
    motion,
    lame,
    shear,
    lame_change,
    shear_change,
    up_rows,
    low_rows,
    up_cols,
    low_cols,
    new_velocity,
    new_stress,
    terms,
):
    _, waves, _, rows, _, _ = motion.shape
    step = pl.program_id(0)

    @pl.when(step == 0)
    def _():
        terms[...] = jnp.zeros(terms.shape, jnp.float32)

    def modulus(strain, first, second, twice):
        trace = first * (strain[0] + strain[1] + strain[2])
        return [trace + twice * strain[i] for i in range(3)] + [
            second * strain[i] for i in range(3, 6)
        ]

    def row(x, carry):
        after = lax.rem(x + 1, rows)
        before = lax.rem(x + rows - 1, rows)
        last, first = x == rows - 1, x == 0
        strain = []
        for w in range(waves):
            vx, vy, vz = motion[0, w, 0, x], motion[0, w, 1, x], motion[0, w, 2, x]
            if w > 0:
                new_velocity[0, w - 1, 0, x] = vx
                new_velocity[0, w - 1, 1, x] = vy
                new_velocity[0, w - 1, 2, x] = vz
            vx_before = jnp.where(first, low_rows[0, w], motion[0, w, 0, before])
            vy_after = jnp.where(last, up_rows[0, w, 0], motion[0, w, 1, after])
            vz_after = jnp.where(last, up_rows[0, w, 1], motion[0, w, 2, after])
            vx_halo = up_cols[0, w, 0, pl.ds(x, 1), :]
            vz_halo = up_cols[0, w, 1, pl.ds(x, 1), :]
            vy_halo = low_cols[0, w, pl.ds(x, 1), :]
            strain.append(
                (
                    vx - vx_before,
                    vy - shifted_down(vy, vy_halo, 0),
                    vz - shifted_down(vz, 0.0, 1),
                    (shifted_up(vx, vx_halo, 0) - vx) + (vy_after - vy),
                    (shifted_up(vx, 0.0, 1) - vx) + (vz_after - vz),
                    (shifted_up(vy, 0.0, 1) - vy) + (shifted_up(vz, vz_halo, 0) - vz),
                )
            )
        first_modulus, second_modulus = lame[x], shear[x]
        twice = 2.0 * second_modulus
        second_change = shear_change[x]
        born = modulus(strain[1], first_modulus, second_modulus, twice)
        changed = modulus(strain[0], lame_change[x], second_change, 2.0 * second_change)
        adjoint = modulus(strain[2], first_modulus, second_modulus, twice)
        a = []
        for c in range(6):
            new_stress[0, 0, c, x] = stress[0, 1, c, x] + COURANT * (born[c] + changed[c])
            value = stress[0, 2, c, x] + COURANT * adjoint[c]
            new_stress[0, 1, c, x] = value
            a.append(value)
        e = strain[0]
        terms[0, x] += (e[0] + e[1] + e[2]) * (a[0] + a[1] + a[2])
        terms[1, x] += (
            2.0 * (e[0] * a[0] + e[1] * a[1] + e[2] * a[2])
            + e[3] * a[3]
            + e[4] * a[4]
            + e[5] * a[5]
        )
        return carry

    lax.fori_loop(0, rows, row, 0)


def share_kernel(
    total_shots, terms, density_term, kernels, landed, landed_density, send_sem, recv_sem
):
    me, count = lax.axis_index("shot"), lax.axis_size("shot")
    rows = kernels.shape[1]
    barrier = pltpu.get_barrier_semaphore()
    for k in range(1, count):
        peer = lax.rem(me + k, count)
        pl.semaphore_signal(barrier, inc=1, device_id={"shot": peer}, device_id_type=MESH)
    pl.semaphore_wait(barrier, count - 1)
    copies = []
    for k in range(1, count):
        peer = lax.rem(me + k, count)
        own = pl.ds(peer * rows, rows)
        for which, (src, dst) in enumerate(
            (
                (terms.at[:, own], landed.at[k - 1]),
                (density_term.at[own], landed_density.at[k - 1]),
            )
        ):
            copy = pltpu.make_async_remote_copy(
                src_ref=src,
                dst_ref=dst,
                send_sem=send_sem.at[k - 1, which],
                recv_sem=recv_sem.at[k - 1, which],
                device_id={"shot": peer},
                device_id_type=MESH,
            )
            copy.start()
            copies.append(copy)
    mine = pl.ds(me * rows, rows)
    total, total_density = terms[:, mine], density_term[mine]
    for k in range(1, count):
        copies[2 * k - 2].wait_recv()
        copies[2 * k - 1].wait_recv()
        total = total + landed[k - 1]
        total_density = total_density + landed_density[k - 1]
    kernels[pl.ds(0, 2)] = total * (1.0 / total_shots)
    kernels[2] = total_density * (1.0 / total_shots)
    for copy in copies:
        copy.wait_send()


def vmem():
    return pl.BlockSpec(memory_space=pltpu.VMEM)


def shards(
    stress_fields,
    velocity_fields,
    lame,
    shear,
    density,
    lame_change,
    shear_change,
    density_change,
    source_cell,
    source_amp,
    receiver_cell,
):
    rows, cols, depth = lame.shape
    shots, waves = stress_fields.shape[:2]
    groups = lax.axis_size("shot")
    every_column = cols * lax.axis_size("gy")
    f32 = jnp.float32
    hbm = pl.BlockSpec(memory_space=pl.ANY)
    smem = pl.BlockSpec(memory_space=pltpu.SMEM)
    transfers = 2 + 6 * shots
    shape = lambda *dims: jax.ShapeDtypeStruct(dims, f32)
    motion, density_term, up_rows, low_rows, up_cols, low_cols = pl.pallas_call(
        functools.partial(motion_kernel, every_column),
        name="motion",
        out_shape=(
            shape(shots, waves, 3, rows, cols, depth),
            shape(rows, cols, depth),
            shape(shots, waves, 2, cols, depth),
            shape(shots, waves, cols, depth),
            shape(shots, waves, 2, rows, depth),
            shape(shots, waves, rows, depth),
        ),
        in_specs=[hbm, hbm, vmem(), vmem(), smem, smem, vmem()],
        out_specs=(hbm, vmem(), vmem(), vmem(), vmem(), vmem()),
        scratch_shapes=[
            pltpu.VMEM((shots, waves, 6, rows, cols, depth), f32),
            pltpu.VMEM((shots, waves, 3, rows, cols, depth), f32),
            pltpu.VMEM((shots, rows, cols, depth), f32),
            pltpu.VMEM((shots, waves, cols, depth), f32),
            pltpu.VMEM((shots, waves, 2, cols, depth), f32),
            pltpu.VMEM((shots, waves, rows, depth), f32),
            pltpu.VMEM((shots, waves, 2, rows, depth), f32),
            pltpu.VMEM((shots, waves, rows, depth), f32),
            pltpu.VMEM((shots, waves, 2, rows, depth), f32),
            pltpu.VMEM((shots, waves, 2, rows, depth), f32),
            pltpu.VMEM((shots, waves, rows, depth), f32),
            pltpu.SemaphoreType.DMA((shots, 2)),
            pltpu.SemaphoreType.DMA((shots,)),
            pltpu.SemaphoreType.DMA((transfers,)),
            pltpu.SemaphoreType.DMA((transfers,)),
        ],
        compiler_params=pltpu.CompilerParams(collective_id=0, has_side_effects=True),
    )(
        stress_fields,
        velocity_fields,
        density,
        density_change,
        source_cell,
        source_amp,
        receiver_cell,
    )

    def per_shot(array):
        rest = array.ndim - 1
        return pl.BlockSpec((1,) + array.shape[1:], lambda s: (s,) + (0,) * rest)

    whole = pl.BlockSpec((rows, cols, depth), lambda s: (0, 0, 0))
    new_velocity, new_stress, terms = pl.pallas_call(
        stress_kernel,
        name="stress",
        grid=(shots,),
        out_shape=(
            shape(shots, 2, 3, rows, cols, depth),
            shape(shots, 2, 6, rows, cols, depth),
            shape(2, rows, cols, depth),
        ),
        in_specs=[
            per_shot(stress_fields),
            per_shot(motion),
            whole,
            whole,
            whole,
            whole,
            per_shot(up_rows),
            per_shot(low_rows),
            per_shot(up_cols),
            per_shot(low_cols),
        ],
        out_specs=(
            pl.BlockSpec((1, 2, 3, rows, cols, depth), lambda s: (s, 0, 0, 0, 0, 0)),
            pl.BlockSpec((1, 2, 6, rows, cols, depth), lambda s: (s, 0, 0, 0, 0, 0)),
            pl.BlockSpec((2, rows, cols, depth), lambda s: (0, 0, 0, 0)),
        ),
    )(
        stress_fields,
        motion,
        lame,
        shear,
        lame_change,
        shear_change,
        up_rows,
        low_rows,
        up_cols,
        low_cols,
    )
    own = rows // groups
    kernels = pl.pallas_call(
        functools.partial(share_kernel, shots * groups),
        name="share",
        out_shape=shape(3, own, cols, depth),
        in_specs=[vmem(), vmem()],
        out_specs=vmem(),
        scratch_shapes=[
            pltpu.VMEM((groups - 1, 2, own, cols, depth), f32),
            pltpu.VMEM((groups - 1, own, cols, depth), f32),
            pltpu.SemaphoreType.DMA((groups - 1, 2)),
            pltpu.SemaphoreType.DMA((groups - 1, 2)),
        ],
        compiler_params=pltpu.CompilerParams(collective_id=1, has_side_effects=True),
    )(terms, density_term)
    return new_velocity, new_stress, kernels


def solution(mesh):
    return jax.shard_map(
        shards,
        mesh=mesh,
        in_specs=(
            P("shot", None, None, "gx", "gy", None),
            P("shot", None, None, "gx", "gy", None),
            P("gx", "gy", None),
            P("gx", "gy", None),
            P("gx", "gy", None),
            P("gx", "gy", None),
            P("gx", "gy", None),
            P("gx", "gy", None),
            P("shot"),
            P("shot"),
            P("shot", None),
        ),
        out_specs=(
            P("shot", None, None, "gx", "gy", None),
            P("shot", None, None, "gx", "gy", None),
            P(None, ("gx", "shot"), "gy", None),
        ),
        check_vma=False,
    )
```

```python
import functools

import jax
import jax.numpy as jnp
from jax import lax
from jax.experimental import pallas as pl
from jax.experimental.pallas import tpu as pltpu
from jax.sharding import PartitionSpec as P

RDEPTH = 2
COURANT = 0.25
MESH = pl.DeviceIdType.MESH
VMEM_LIMIT = 32 * 1024 * 1024


def shifted_up(tile, halo, axis):
    length = tile.shape[axis]
    index = lax.broadcasted_iota(jnp.int32, tile.shape, axis)
    return jnp.where(index == length - 1, halo, pltpu.roll(tile, length - 1, axis))


def shifted_down(tile, halo, axis):
    index = lax.broadcasted_iota(jnp.int32, tile.shape, axis)
    return jnp.where(index == 0, halo, pltpu.roll(tile, 1, axis))


def step_kernel(
    every_column,
    total_shots,
    stress,
    velocity,
    lame_in,
    shear_in,
    density_in,
    lame_change_in,
    shear_change_in,
    density_change_in,
    receivers_in,
    source_cell,
    source_amp,
    st,
    mo,
    kernels,
    params,
    receivers,
    record,
    accel0,
    strain0,
    terms,
    st_up_rows,
    st_low_rows,
    st_up_cols,
    st_low_cols,
    st_up_cols_out,
    st_low_cols_out,
    up_rows,
    low_rows,
    up_cols,
    low_cols,
    up_cols_out,
    low_cols_out,
    landed,
    load_sem,
    param_sem,
    send_sem,
    recv_sem,
    share_send_sem,
    share_recv_sem,
):
    shots, waves, _, rows, cols, depth = stress.shape
    gx, gy = lax.axis_index("gx"), lax.axis_index("gy")
    nx, ny = lax.axis_size("gx"), lax.axis_size("gy")
    me, groups = lax.axis_index("shot"), lax.axis_size("shot")
    own = rows // groups
    has_low_x, has_up_x = gx > 0, gx < nx - 1
    has_low_y, has_up_y = gy > 0, gy < ny - 1
    sides = (
        (has_low_x, {"gx": gx - 1}),
        (has_up_x, {"gx": gx + 1}),
        (has_low_y, {"gy": gy - 1}),
        (has_up_y, {"gy": gy + 1}),
    )
    barrier = pltpu.get_barrier_semaphore()
    for present, device in sides:

        @pl.when(present)
        def _(device=device):
            pl.semaphore_signal(barrier, inc=1, device_id=device, device_id_type=MESH)

    for k in range(1, groups):
        peer = lax.rem(me + k, groups)
        pl.semaphore_signal(barrier, inc=1, device_id={"shot": peer}, device_id_type=MESH)

    stress_loads = [
        pltpu.make_async_copy(stress.at[s], st.at[s], load_sem.at[s, 0]) for s in range(shots)
    ]
    motion_loads = [
        pltpu.make_async_copy(velocity.at[s], mo.at[s], load_sem.at[s, 1]) for s in range(shots)
    ]
    receiver_load = pltpu.make_async_copy(receivers_in, receivers, param_sem.at[6])
    sources = (density_in, density_change_in, lame_in, shear_in, lame_change_in, shear_change_in)
    param_loads = [
        pltpu.make_async_copy(source, params.at[i], param_sem.at[i])
        for i, source in enumerate(sources)
    ]
    stress_loads[0].start()
    receiver_load.start()
    for copy in stress_loads[1:] + param_loads[:2] + motion_loads + param_loads[2:]:
        copy.start()
    density, density_change, lame, shear, lame_change, shear_change = (
        params.at[i] for i in range(6)
    )

    def face(src, dst, slot, device):
        return pltpu.make_async_remote_copy(
            src_ref=src,
            dst_ref=dst,
            send_sem=send_sem.at[slot],
            recv_sem=recv_sem.at[slot],
            device_id=device,
            device_id_type=MESH,
        )

    low_x, up_x, low_y, up_y = (device for _, device in sides)
    stress_faces, motion_faces = [], []
    for s in range(shots):
        slot = 8 * s
        stress_faces.append(
            (
                (face(stress.at[s, :, 0, 0], st_up_rows.at[s], slot, low_x), has_low_x, has_up_x),
                (
                    face(stress.at[s, :, pl.ds(3, 2), rows - 1], st_low_rows.at[s], slot + 1, up_x),
                    has_up_x,
                    has_low_x,
                ),
                (face(st_up_cols_out.at[s], st_up_cols.at[s], slot + 2, low_y), has_low_y, has_up_y),
                (
                    face(st_low_cols_out.at[s], st_low_cols.at[s], slot + 3, up_y),
                    has_up_y,
                    has_low_y,
                ),
            )
        )
        motion_faces.append(
            (
                (
                    face(mo.at[s, :, pl.ds(1, 2), 0], up_rows.at[s], slot + 4, low_x),
                    has_low_x,
                    has_up_x,
                ),
                (face(mo.at[s, :, 0, rows - 1], low_rows.at[s], slot + 5, up_x), has_up_x, has_low_x),
                (face(up_cols_out.at[s], up_cols.at[s], slot + 6, low_y), has_low_y, has_up_y),
                (face(low_cols_out.at[s], low_cols.at[s], slot + 7, up_y), has_up_y, has_low_y),
            )
        )

    def send(faces):
        for copy, sends, _ in faces:

            @pl.when(sends)
            def _(copy=copy):
                copy.start()

    def sent(faces):
        for copy, sends, _ in faces:

            @pl.when(sends)
            def _(copy=copy):
                copy.wait_send()

    neighbours = groups - 1
    for present, _ in sides:
        neighbours = neighbours + present.astype(jnp.int32)
    pl.semaphore_wait(barrier, neighbours)
    for s in range(shots):
        send(stress_faces[s][:2])
    row_start, col_start = gx * rows, gy * cols

    for s in range(shots):
        stress_loads[s].wait()
        for w in range(waves):
            st_up_cols_out[s, w] = st[s, w, 1, :, 0, :]
            st_low_cols_out[s, w, 0] = st[s, w, 3, :, cols - 1, :]
            st_low_cols_out[s, w, 1] = st[s, w, 5, :, cols - 1, :]
        send(stress_faces[s][2:])

    receiver_load.wait()
    count = receivers.shape[1]
    plane = (lax.broadcasted_iota(jnp.int32, (count, depth), 1) == RDEPTH).astype(jnp.bfloat16)
    cell = (
        lax.broadcasted_iota(jnp.int32, (rows, cols, count), 0) + row_start
    ) * every_column + (lax.broadcasted_iota(jnp.int32, (rows, cols, count), 1) + col_start)
    cell = cell.reshape(rows * cols, count)
    for s in range(shots):
        marks = jnp.where(receivers[pl.ds(s, 1), :] == cell, 1.0, 0.0).astype(jnp.bfloat16)
        field = jnp.dot(marks, plane, preferred_element_type=jnp.float32)
        record[s] = field.reshape(rows, cols, depth)

    place = (
        lax.broadcasted_iota(jnp.int32, (cols, depth), 0) + col_start
    ) * depth + lax.broadcasted_iota(jnp.int32, (cols, depth), 1)
    param_loads[0].wait()
    param_loads[1].wait()

    for s in range(shots):
        motion_loads[s].wait()
        target, amplitude = source_cell[s], source_amp[s]

        def motion_row(x, carry, s=s, target=target, amplitude=amplitude):
            after = lax.rem(x + 1, rows)
            before = lax.rem(x + rows - 1, rows)
            last, first = x == rows - 1, x == 0
            buoyancy = 1.0 / density[x]
            scaled = COURANT * buoyancy
            change = density_change[x] * buoyancy
            accel = []
            for w in range(waves):
                sxx, syy, szz = st[s, w, 0, x], st[s, w, 1, x], st[s, w, 2, x]
                sxy, sxz, syz = st[s, w, 3, x], st[s, w, 4, x], st[s, w, 5, x]
                sxx_after = jnp.where(last, 0.0, st[s, w, 0, after])
                sxy_before = jnp.where(first, 0.0, st[s, w, 3, before])
                sxz_before = jnp.where(first, 0.0, st[s, w, 4, before])
                accel.append(
                    (
                        (sxx_after - sxx)
                        + (sxy - shifted_down(sxy, 0.0, 0))
                        + (sxz - shifted_down(sxz, 0.0, 1)),
                        (sxy - sxy_before)
                        + (shifted_up(syy, 0.0, 0) - syy)
                        + (syz - shifted_down(syz, 0.0, 1)),
                        (sxz - sxz_before)
                        + (syz - shifted_down(syz, 0.0, 0))
                        + (shifted_up(szz, 0.0, 1) - szz),
                    )
                )
            here = place + (x + row_start) * (every_column * depth)
            source = jnp.where(here == target, amplitude, 0.0)
            for c in range(3):
                first_wave = mo[s, 0, c, x] + scaled * accel[0][c]
                born = mo[s, 1, c, x] + scaled * (accel[1][c] - change * accel[0][c])
                adjoint = mo[s, 2, c, x] + scaled * accel[2][c]
                if c == 2:
                    first_wave = first_wave + scaled * source
                    adjoint = adjoint + scaled * record[s, x] * born
                accel0[s, c, x] = accel[0][c]
                mo[s, 0, c, x] = first_wave
                mo[s, 1, c, x] = born
                mo[s, 2, c, x] = adjoint
            return carry

        lax.fori_loop(0, rows, motion_row, 0)

    every = slice(None)
    low_face, up_face = (0, every), (rows - 1, every)
    left_face, right_face = (every, 0), (every, cols - 1)

    def fix_motion(s, where, c, halo, sign):
        at = where + (every,)
        buoyancy = 1.0 / density[at]
        scaled = COURANT * buoyancy
        change = density_change[at] * buoyancy
        d0, d1, d2 = (sign * halo[w] for w in range(waves))
        accel0[(s, c) + at] += d0
        mo[(s, 0, c) + at] += scaled * d0
        born = scaled * (d1 - change * d0)
        mo[(s, 1, c) + at] += born
        adjoint = scaled * d2
        if c == 2:
            adjoint = adjoint + scaled * record[(s,) + at] * born
        mo[(s, 2, c) + at] += adjoint

    def layers(ref, s, which=None):
        if which is None:
            return [ref[s, w] for w in range(waves)]
        return [ref[s, w, which] for w in range(waves)]

    for s in range(shots):
        (up_x_copy, _, up_x_in), (low_x_copy, _, low_x_in), (up_y_copy, _, up_y_in), (
            low_y_copy,
            _,
            low_y_in,
        ) = stress_faces[s]

        @pl.when(up_x_in)
        def _(s=s, copy=up_x_copy):
            copy.wait_recv()
            fix_motion(s, up_face, 0, layers(st_up_rows, s), 1.0)

        @pl.when(low_x_in)
        def _(s=s, copy=low_x_copy):
            copy.wait_recv()
            fix_motion(s, low_face, 1, layers(st_low_rows, s, 0), -1.0)
            fix_motion(s, low_face, 2, layers(st_low_rows, s, 1), -1.0)

        @pl.when(up_y_in)
        def _(s=s, copy=up_y_copy):
            copy.wait_recv()
            fix_motion(s, right_face, 1, layers(st_up_cols, s), 1.0)

        @pl.when(low_y_in)
        def _(s=s, copy=low_y_copy):
            copy.wait_recv()
            fix_motion(s, left_face, 0, layers(st_low_cols, s, 0), -1.0)
            fix_motion(s, left_face, 2, layers(st_low_cols, s, 1), -1.0)

        send(motion_faces[s][:2])
        for w in range(waves):
            up_cols_out[s, w, 0] = mo[s, w, 0, :, 0, :]
            up_cols_out[s, w, 1] = mo[s, w, 2, :, 0, :]
            low_cols_out[s, w] = mo[s, w, 1, :, cols - 1, :]
        send(motion_faces[s][2:])

    for copy in param_loads[2:]:
        copy.wait()

    def modulus(strain, first, second, twice):
        trace = first * (strain[0] + strain[1] + strain[2])
        return [trace + twice * strain[i] for i in range(3)] + [
            second * strain[i] for i in range(3, 6)
        ]

    for s in range(shots):

        def stress_row(x, carry, s=s):
            after = lax.rem(x + 1, rows)
            before = lax.rem(x + rows - 1, rows)
            last, first = x == rows - 1, x == 0
            strain, adjoint_motion = [], None
            for w in range(waves):
                vx, vy, vz = mo[s, w, 0, x], mo[s, w, 1, x], mo[s, w, 2, x]
                adjoint_motion = (vx, vy, vz)
                vx_before = jnp.where(first, 0.0, mo[s, w, 0, before])
                vy_after = jnp.where(last, 0.0, mo[s, w, 1, after])
                vz_after = jnp.where(last, 0.0, mo[s, w, 2, after])
                strain.append(
                    (
                        vx - vx_before,
                        vy - shifted_down(vy, 0.0, 0),
                        vz - shifted_down(vz, 0.0, 1),
                        (shifted_up(vx, 0.0, 0) - vx) + (vy_after - vy),
                        (shifted_up(vx, 0.0, 1) - vx) + (vz_after - vz),
                        (shifted_up(vy, 0.0, 1) - vy) + (shifted_up(vz, 0.0, 0) - vz),
                    )
                )
            first_modulus, second_modulus = lame[x], shear[x]
            twice = 2.0 * second_modulus
            second_change = shear_change[x]
            born = modulus(strain[1], first_modulus, second_modulus, twice)
            changed = modulus(strain[0], lame_change[x], second_change, 2.0 * second_change)
            adjoint = modulus(strain[2], first_modulus, second_modulus, twice)
            for c in range(6):
                strain0[s, c, x] = strain[0][c]
                st[s, 1, c, x] = st[s, 1, c, x] + COURANT * (born[c] + changed[c])
                st[s, 2, c, x] = st[s, 2, c, x] + COURANT * adjoint[c]
            total = (
                accel0[s, 0, x] * adjoint_motion[0]
                + accel0[s, 1, x] * adjoint_motion[1]
                + accel0[s, 2, x] * adjoint_motion[2]
            )
            total = (1.0 / density[x]) * total
            terms[2, x] = total if s == 0 else terms[2, x] + total
            return carry

        lax.fori_loop(0, rows, stress_row, 0)

    def fix_stress(s, where, c, halo, sign):
        at = where + (every,)
        d0, d1, d2 = (sign * halo[w] for w in range(waves))
        strain0[(s, c) + at] += d0
        second = shear[at]
        own_born = second * d1 + shear_change[at] * d0
        own_adjoint = second * d2
        if c >= 3:
            st[(s, 1, c) + at] += COURANT * own_born
            st[(s, 2, c) + at] += COURANT * own_adjoint
            return
        born = lame[at] * d1 + lame_change[at] * d0
        adjoint = lame[at] * d2
        for i in range(3):
            more_born, more_adjoint = born, adjoint
            if i == c:
                more_born, more_adjoint = born + 2.0 * own_born, adjoint + 2.0 * own_adjoint
            st[(s, 1, i) + at] += COURANT * more_born
            st[(s, 2, i) + at] += COURANT * more_adjoint

    for s in range(shots):
        (up_x_copy, _, up_x_in), (low_x_copy, _, low_x_in), (up_y_copy, _, up_y_in), (
            low_y_copy,
            _,
            low_y_in,
        ) = motion_faces[s]

        @pl.when(low_x_in)
        def _(s=s, copy=low_x_copy):
            copy.wait_recv()
            fix_stress(s, low_face, 0, layers(low_rows, s), -1.0)

        @pl.when(up_x_in)
        def _(s=s, copy=up_x_copy):
            copy.wait_recv()
            fix_stress(s, up_face, 3, layers(up_rows, s, 0), 1.0)
            fix_stress(s, up_face, 4, layers(up_rows, s, 1), 1.0)

        @pl.when(low_y_in)
        def _(s=s, copy=low_y_copy):
            copy.wait_recv()
            fix_stress(s, left_face, 1, layers(low_cols, s), -1.0)

        @pl.when(up_y_in)
        def _(s=s, copy=up_y_copy):
            copy.wait_recv()
            fix_stress(s, right_face, 3, layers(up_cols, s, 0), 1.0)
            fix_stress(s, right_face, 5, layers(up_cols, s, 1), 1.0)

    def term_row(x, carry):
        trace_sum, shear_sum = None, None
        for s in range(shots):
            e = [strain0[s, c, x] for c in range(6)]
            a = [st[s, 2, c, x] for c in range(6)]
            trace = (e[0] + e[1] + e[2]) * (a[0] + a[1] + a[2])
            product = (
                2.0 * (e[0] * a[0] + e[1] * a[1] + e[2] * a[2])
                + e[3] * a[3]
                + e[4] * a[4]
                + e[5] * a[5]
            )
            trace_sum = trace if s == 0 else trace_sum + trace
            shear_sum = product if s == 0 else shear_sum + product
        terms[0, x] = trace_sum
        terms[1, x] = shear_sum
        return carry

    shares = []
    for k in range(1, groups):
        peer = lax.rem(me + k, groups)
        lax.fori_loop(0, own, lambda i, carry, peer=peer: term_row(peer * own + i, carry), 0)
        copy = pltpu.make_async_remote_copy(
            src_ref=terms.at[:, pl.ds(peer * own, own)],
            dst_ref=landed.at[k - 1],
            send_sem=share_send_sem.at[k - 1],
            recv_sem=share_recv_sem.at[k - 1],
            device_id={"shot": peer},
            device_id_type=MESH,
        )
        copy.start()
        shares.append(copy)
    lax.fori_loop(0, own, lambda i, carry: term_row(me * own + i, carry), 0)
    for copy in shares:
        copy.wait_recv()
    total = terms[:, pl.ds(me * own, own)]
    for k in range(1, groups):
        total = total + landed[k - 1]
    kernels[...] = total * (1.0 / total_shots)
    for s in range(shots):
        sent(stress_faces[s])
        sent(motion_faces[s])
    for copy in shares:
        copy.wait_send()


def write_kernel(st, mo, kernels_in, new_velocity, new_stress, kernels, sems):
    shots = st.shape[0]
    copies = [pltpu.make_async_copy(kernels_in, kernels, sems.at[2 * shots])]
    for s in range(shots):
        copies.append(
            pltpu.make_async_copy(st.at[s, pl.ds(1, 2)], new_stress.at[s], sems.at[2 * s])
        )
        copies.append(
            pltpu.make_async_copy(mo.at[s, pl.ds(1, 2)], new_velocity.at[s], sems.at[2 * s + 1])
        )
    for copy in copies:
        copy.start()
    for copy in copies:
        copy.wait()


def shards(
    stress_fields,
    velocity_fields,
    lame,
    shear,
    density,
    lame_change,
    shear_change,
    density_change,
    source_cell,
    source_amp,
    receiver_cell,
):
    rows, cols, depth = lame.shape
    shots, waves = stress_fields.shape[:2]
    groups = lax.axis_size("shot")
    own = rows // groups
    every_column = cols * lax.axis_size("gy")
    f32 = jnp.float32
    hbm = pl.BlockSpec(memory_space=pltpu.HBM)
    smem = pl.BlockSpec(memory_space=pltpu.SMEM)
    vmem = pl.BlockSpec(memory_space=pltpu.VMEM)
    face_rows = [(shots, waves, cols, depth), (shots, waves, 2, cols, depth)]
    face_cols = [(shots, waves, rows, depth), (shots, waves, 2, rows, depth)]
    scratch = [
        (6, rows, cols, depth),
        None,
        (shots, rows, cols, depth),
        (shots, 3, rows, cols, depth),
        (shots, 6, rows, cols, depth),
        (3, rows, cols, depth),
        face_rows[0],
        face_rows[1],
        face_cols[0],
        face_cols[1],
        face_cols[0],
        face_cols[1],
        face_rows[1],
        face_rows[0],
        face_cols[1],
        face_cols[0],
        face_cols[1],
        face_cols[0],
        (max(groups - 1, 1), 3, own, cols, depth),
    ]
    scratch = [
        pltpu.VMEM(receiver_cell.shape, jnp.int32) if dims is None else pltpu.VMEM(dims, f32)
        for dims in scratch
    ]
    st, mo, kernels = pl.pallas_call(
        functools.partial(step_kernel, every_column, shots * groups),
        name="step",
        out_shape=(
            pltpu.VMEM((shots, waves, 6, rows, cols, depth), f32),
            pltpu.VMEM((shots, waves, 3, rows, cols, depth), f32),
            pltpu.VMEM((3, own, cols, depth), f32),
        ),
        in_specs=[hbm] * 9 + [smem] * 2,
        out_specs=(vmem, vmem, vmem),
        scratch_shapes=scratch
        + [
            pltpu.SemaphoreType.DMA((shots, 2)),
            pltpu.SemaphoreType.DMA((7,)),
            pltpu.SemaphoreType.DMA((8 * shots,)),
            pltpu.SemaphoreType.DMA((8 * shots,)),
            pltpu.SemaphoreType.DMA((max(groups - 1, 1),)),
            pltpu.SemaphoreType.DMA((max(groups - 1, 1),)),
        ],
        compiler_params=pltpu.CompilerParams(
            collective_id=0, has_side_effects=True, vmem_limit_bytes=VMEM_LIMIT
        ),
    )(
        *(
            pltpu.with_memory_space_constraint(array, pltpu.HBM)
            for array in (
                stress_fields,
                velocity_fields,
                lame,
                shear,
                density,
                lame_change,
                shear_change,
                density_change,
                receiver_cell,
                source_cell,
                source_amp,
            )
        ),
    )
    shape = lambda *dims: jax.ShapeDtypeStruct(dims, f32)
    return pl.pallas_call(
        write_kernel,
        name="write",
        out_shape=(
            shape(shots, 2, 3, rows, cols, depth),
            shape(shots, 2, 6, rows, cols, depth),
            shape(3, own, cols, depth),
        ),
        in_specs=[vmem] * 3,
        out_specs=(hbm, hbm, hbm),
        scratch_shapes=[pltpu.SemaphoreType.DMA((2 * shots + 1,))],
        compiler_params=pltpu.CompilerParams(vmem_limit_bytes=VMEM_LIMIT),
    )(st, mo, kernels)


def solution(mesh):
    return jax.shard_map(
        shards,
        mesh=mesh,
        in_specs=(
            P("shot", None, None, "gx", "gy", None),
            P("shot", None, None, "gx", "gy", None),
            P("gx", "gy", None),
            P("gx", "gy", None),
            P("gx", "gy", None),
            P("gx", "gy", None),
            P("gx", "gy", None),
            P("gx", "gy", None),
            P("shot"),
            P("shot"),
            P("shot", None),
        ),
        out_specs=(
            P("shot", None, None, "gx", "gy", None),
            P("shot", None, None, "gx", "gy", None),
            P(None, ("gx", "shot"), "gy", None),
        ),
        check_vma=False,
    )
```

```python
import functools

import jax
import jax.numpy as jnp
from jax import lax
from jax.experimental import pallas as pl
from jax.experimental.pallas import tpu as pltpu
from jax.sharding import PartitionSpec as P

RDEPTH = 2
COURANT = 0.25
MESH = pl.DeviceIdType.MESH
VMEM_LIMIT = 32 * 1024 * 1024


def shifted_up(tile, halo, axis):
    length = tile.shape[axis]
    index = lax.broadcasted_iota(jnp.int32, tile.shape, axis)
    return jnp.where(index == length - 1, halo, pltpu.roll(tile, length - 1, axis))


def shifted_down(tile, halo, axis):
    index = lax.broadcasted_iota(jnp.int32, tile.shape, axis)
    return jnp.where(index == 0, halo, pltpu.roll(tile, 1, axis))


def step_kernel(
    every_column,
    total_shots,
    stress,
    velocity,
    lame_in,
    shear_in,
    density_in,
    lame_change_in,
    shear_change_in,
    density_change_in,
    receivers_in,
    source_cell,
    source_amp,
    st,
    mo,
    kernels,
    params,
    receivers,
    record,
    accel0,
    strain0,
    terms,
    st_up_rows,
    st_low_rows,
    st_up_cols,
    st_low_cols,
    st_up_cols_out,
    st_low_cols_out,
    up_rows,
    low_rows,
    up_cols,
    low_cols,
    up_cols_out,
    low_cols_out,
    landed,
    load_sem,
    param_sem,
    send_sem,
    recv_sem,
    share_send_sem,
    share_recv_sem,
):
    shots, waves, _, rows, cols, depth = stress.shape
    gx, gy = lax.axis_index("gx"), lax.axis_index("gy")
    nx, ny = lax.axis_size("gx"), lax.axis_size("gy")
    me, groups = lax.axis_index("shot"), lax.axis_size("shot")
    own = rows // groups
    has_low_x, has_up_x = gx > 0, gx < nx - 1
    has_low_y, has_up_y = gy > 0, gy < ny - 1
    sides = (
        (has_low_x, {"gx": gx - 1}),
        (has_up_x, {"gx": gx + 1}),
        (has_low_y, {"gy": gy - 1}),
        (has_up_y, {"gy": gy + 1}),
    )
    barrier = pltpu.get_barrier_semaphore()
    for present, device in sides:

        @pl.when(present)
        def _(device=device):
            pl.semaphore_signal(barrier, inc=1, device_id=device, device_id_type=MESH)

    for k in range(1, groups):
        peer = lax.rem(me + k, groups)
        pl.semaphore_signal(barrier, inc=1, device_id={"shot": peer}, device_id_type=MESH)

    stress_loads = [
        pltpu.make_async_copy(stress.at[s], st.at[s], load_sem.at[s, 0]) for s in range(shots)
    ]
    motion_loads = [
        pltpu.make_async_copy(velocity.at[s], mo.at[s], load_sem.at[s, 1]) for s in range(shots)
    ]
    receiver_load = pltpu.make_async_copy(receivers_in, receivers, param_sem.at[6])
    sources = (density_in, density_change_in, lame_in, shear_in, lame_change_in, shear_change_in)
    param_loads = [
        pltpu.make_async_copy(source, params.at[i], param_sem.at[i])
        for i, source in enumerate(sources)
    ]
    stress_loads[0].start()
    receiver_load.start()
    for copy in stress_loads[1:] + param_loads[:2] + motion_loads + param_loads[2:]:
        copy.start()
    density, density_change, lame, shear, lame_change, shear_change = (
        params.at[i] for i in range(6)
    )

    def face(src, dst, slot, device):
        return pltpu.make_async_remote_copy(
            src_ref=src,
            dst_ref=dst,
            send_sem=send_sem.at[slot],
            recv_sem=recv_sem.at[slot],
            device_id=device,
            device_id_type=MESH,
        )

    low_x, up_x, low_y, up_y = (device for _, device in sides)
    stress_faces, motion_faces = [], []
    for s in range(shots):
        slot = 8 * s
        stress_faces.append(
            (
                (face(stress.at[s, :, 0, 0], st_up_rows.at[s], slot, low_x), has_low_x, has_up_x),
                (
                    face(stress.at[s, :, pl.ds(3, 2), rows - 1], st_low_rows.at[s], slot + 1, up_x),
                    has_up_x,
                    has_low_x,
                ),
                (face(st_up_cols_out.at[s], st_up_cols.at[s], slot + 2, low_y), has_low_y, has_up_y),
                (
                    face(st_low_cols_out.at[s], st_low_cols.at[s], slot + 3, up_y),
                    has_up_y,
                    has_low_y,
                ),
            )
        )
        motion_faces.append(
            (
                (
                    face(mo.at[s, :, pl.ds(1, 2), 0], up_rows.at[s], slot + 4, low_x),
                    has_low_x,
                    has_up_x,
                ),
                (face(mo.at[s, :, 0, rows - 1], low_rows.at[s], slot + 5, up_x), has_up_x, has_low_x),
                (face(up_cols_out.at[s], up_cols.at[s], slot + 6, low_y), has_low_y, has_up_y),
                (face(low_cols_out.at[s], low_cols.at[s], slot + 7, up_y), has_up_y, has_low_y),
            )
        )

    def send(faces):
        for copy, sends, _ in faces:

            @pl.when(sends)
            def _(copy=copy):
                copy.start()

    def sent(faces):
        for copy, sends, _ in faces:

            @pl.when(sends)
            def _(copy=copy):
                copy.wait_send()

    neighbours = groups - 1
    for present, _ in sides:
        neighbours = neighbours + present.astype(jnp.int32)
    pl.semaphore_wait(barrier, neighbours)
    for s in range(shots):
        send(stress_faces[s][:2])
    row_start, col_start = gx * rows, gy * cols

    for s in range(shots):
        stress_loads[s].wait()
        for w in range(waves):
            st_up_cols_out[s, w] = st[s, w, 1, :, 0, :]
            st_low_cols_out[s, w, 0] = st[s, w, 3, :, cols - 1, :]
            st_low_cols_out[s, w, 1] = st[s, w, 5, :, cols - 1, :]
        send(stress_faces[s][2:])

    receiver_load.wait()
    count = receivers.shape[1]
    plane = (lax.broadcasted_iota(jnp.int32, (count, depth), 1) == RDEPTH).astype(jnp.bfloat16)
    cell = (
        lax.broadcasted_iota(jnp.int32, (rows, cols, count), 0) + row_start
    ) * every_column + (lax.broadcasted_iota(jnp.int32, (rows, cols, count), 1) + col_start)
    cell = cell.reshape(rows * cols, count)
    for s in range(shots):
        marks = jnp.where(receivers[pl.ds(s, 1), :] == cell, 1.0, 0.0).astype(jnp.bfloat16)
        field = jnp.dot(marks, plane, preferred_element_type=jnp.float32)
        record[s] = field.reshape(rows, cols, depth)

    place = (
        lax.broadcasted_iota(jnp.int32, (cols, depth), 0) + col_start
    ) * depth + lax.broadcasted_iota(jnp.int32, (cols, depth), 1)
    param_loads[0].wait()
    param_loads[1].wait()

    for s in range(shots):
        motion_loads[s].wait()
        target, amplitude = source_cell[s], source_amp[s]

        def motion_row(x, carry, s=s, target=target, amplitude=amplitude):
            after = lax.rem(x + 1, rows)
            before = lax.rem(x + rows - 1, rows)
            last, first = x == rows - 1, x == 0
            buoyancy = 1.0 / density[x]
            scaled = COURANT * buoyancy
            change = density_change[x] * buoyancy
            accel = []
            for w in range(waves):
                sxx, syy, szz = st[s, w, 0, x], st[s, w, 1, x], st[s, w, 2, x]
                sxy, sxz, syz = st[s, w, 3, x], st[s, w, 4, x], st[s, w, 5, x]
                sxx_after = jnp.where(last, 0.0, st[s, w, 0, after])
                sxy_before = jnp.where(first, 0.0, st[s, w, 3, before])
                sxz_before = jnp.where(first, 0.0, st[s, w, 4, before])
                accel.append(
                    (
                        (sxx_after - sxx)
                        + (sxy - shifted_down(sxy, 0.0, 0))
                        + (sxz - shifted_down(sxz, 0.0, 1)),
                        (sxy - sxy_before)
                        + (shifted_up(syy, 0.0, 0) - syy)
                        + (syz - shifted_down(syz, 0.0, 1)),
                        (sxz - sxz_before)
                        + (syz - shifted_down(syz, 0.0, 0))
                        + (shifted_up(szz, 0.0, 1) - szz),
                    )
                )
            here = place + (x + row_start) * (every_column * depth)
            source = jnp.where(here == target, amplitude, 0.0)
            for c in range(3):
                first_wave = mo[s, 0, c, x] + scaled * accel[0][c]
                born = mo[s, 1, c, x] + scaled * (accel[1][c] - change * accel[0][c])
                adjoint = mo[s, 2, c, x] + scaled * accel[2][c]
                if c == 2:
                    first_wave = first_wave + scaled * source
                    adjoint = adjoint + scaled * record[s, x] * born
                accel0[s, c, x] = accel[0][c]
                mo[s, 0, c, x] = first_wave
                mo[s, 1, c, x] = born
                mo[s, 2, c, x] = adjoint
            return carry

        lax.fori_loop(0, rows, motion_row, 0, unroll=2)

    every = slice(None)
    low_face, up_face = (0, every), (rows - 1, every)
    left_face, right_face = (every, 0), (every, cols - 1)

    def fix_motion(s, where, c, halo, sign):
        at = where + (every,)
        buoyancy = 1.0 / density[at]
        scaled = COURANT * buoyancy
        change = density_change[at] * buoyancy
        d0, d1, d2 = (sign * halo[w] for w in range(waves))
        accel0[(s, c) + at] += d0
        mo[(s, 0, c) + at] += scaled * d0
        born = scaled * (d1 - change * d0)
        mo[(s, 1, c) + at] += born
        adjoint = scaled * d2
        if c == 2:
            adjoint = adjoint + scaled * record[(s,) + at] * born
        mo[(s, 2, c) + at] += adjoint

    def layers(ref, s, which=None):
        if which is None:
            return [ref[s, w] for w in range(waves)]
        return [ref[s, w, which] for w in range(waves)]

    for s in range(shots):
        (up_x_copy, _, up_x_in), (low_x_copy, _, low_x_in), (up_y_copy, _, up_y_in), (
            low_y_copy,
            _,
            low_y_in,
        ) = stress_faces[s]

        @pl.when(up_x_in)
        def _(s=s, copy=up_x_copy):
            copy.wait_recv()
            fix_motion(s, up_face, 0, layers(st_up_rows, s), 1.0)

        @pl.when(low_x_in)
        def _(s=s, copy=low_x_copy):
            copy.wait_recv()
            fix_motion(s, low_face, 1, layers(st_low_rows, s, 0), -1.0)
            fix_motion(s, low_face, 2, layers(st_low_rows, s, 1), -1.0)

        @pl.when(up_y_in)
        def _(s=s, copy=up_y_copy):
            copy.wait_recv()
            fix_motion(s, right_face, 1, layers(st_up_cols, s), 1.0)

        @pl.when(low_y_in)
        def _(s=s, copy=low_y_copy):
            copy.wait_recv()
            fix_motion(s, left_face, 0, layers(st_low_cols, s, 0), -1.0)
            fix_motion(s, left_face, 2, layers(st_low_cols, s, 1), -1.0)

        send(motion_faces[s][:2])
        for w in range(waves):
            up_cols_out[s, w, 0] = mo[s, w, 0, :, 0, :]
            up_cols_out[s, w, 1] = mo[s, w, 2, :, 0, :]
            low_cols_out[s, w] = mo[s, w, 1, :, cols - 1, :]
        send(motion_faces[s][2:])

    for copy in param_loads[2:]:
        copy.wait()

    def modulus(strain, first, second, twice):
        trace = first * (strain[0] + strain[1] + strain[2])
        return [trace + twice * strain[i] for i in range(3)] + [
            second * strain[i] for i in range(3, 6)
        ]

    for s in range(shots):

        def stress_row(x, carry, s=s):
            after = lax.rem(x + 1, rows)
            before = lax.rem(x + rows - 1, rows)
            last, first = x == rows - 1, x == 0
            strain, adjoint_motion = [], None
            for w in range(waves):
                vx, vy, vz = mo[s, w, 0, x], mo[s, w, 1, x], mo[s, w, 2, x]
                adjoint_motion = (vx, vy, vz)
                vx_before = jnp.where(first, 0.0, mo[s, w, 0, before])
                vy_after = jnp.where(last, 0.0, mo[s, w, 1, after])
                vz_after = jnp.where(last, 0.0, mo[s, w, 2, after])
                strain.append(
                    (
                        vx - vx_before,
                        vy - shifted_down(vy, 0.0, 0),
                        vz - shifted_down(vz, 0.0, 1),
                        (shifted_up(vx, 0.0, 0) - vx) + (vy_after - vy),
                        (shifted_up(vx, 0.0, 1) - vx) + (vz_after - vz),
                        (shifted_up(vy, 0.0, 1) - vy) + (shifted_up(vz, 0.0, 0) - vz),
                    )
                )
            first_modulus, second_modulus = lame[x], shear[x]
            twice = 2.0 * second_modulus
            second_change = shear_change[x]
            born = modulus(strain[1], first_modulus, second_modulus, twice)
            changed = modulus(strain[0], lame_change[x], second_change, 2.0 * second_change)
            adjoint = modulus(strain[2], first_modulus, second_modulus, twice)
            for c in range(6):
                strain0[s, c, x] = strain[0][c]
                st[s, 1, c, x] = st[s, 1, c, x] + COURANT * (born[c] + changed[c])
                st[s, 2, c, x] = st[s, 2, c, x] + COURANT * adjoint[c]
            total = (
                accel0[s, 0, x] * adjoint_motion[0]
                + accel0[s, 1, x] * adjoint_motion[1]
                + accel0[s, 2, x] * adjoint_motion[2]
            )
            total = (1.0 / density[x]) * total
            terms[2, x] = total if s == 0 else terms[2, x] + total
            return carry

        lax.fori_loop(0, rows, stress_row, 0, unroll=2)

    def fix_stress(s, where, c, halo, sign):
        at = where + (every,)
        d0, d1, d2 = (sign * halo[w] for w in range(waves))
        strain0[(s, c) + at] += d0
        second = shear[at]
        own_born = second * d1 + shear_change[at] * d0
        own_adjoint = second * d2
        if c >= 3:
            st[(s, 1, c) + at] += COURANT * own_born
            st[(s, 2, c) + at] += COURANT * own_adjoint
            return
        born = lame[at] * d1 + lame_change[at] * d0
        adjoint = lame[at] * d2
        for i in range(3):
            more_born, more_adjoint = born, adjoint
            if i == c:
                more_born, more_adjoint = born + 2.0 * own_born, adjoint + 2.0 * own_adjoint
            st[(s, 1, i) + at] += COURANT * more_born
            st[(s, 2, i) + at] += COURANT * more_adjoint

    for s in range(shots):
        (up_x_copy, _, up_x_in), (low_x_copy, _, low_x_in), (up_y_copy, _, up_y_in), (
            low_y_copy,
            _,
            low_y_in,
        ) = motion_faces[s]

        @pl.when(low_x_in)
        def _(s=s, copy=low_x_copy):
            copy.wait_recv()
            fix_stress(s, low_face, 0, layers(low_rows, s), -1.0)

        @pl.when(up_x_in)
        def _(s=s, copy=up_x_copy):
            copy.wait_recv()
            fix_stress(s, up_face, 3, layers(up_rows, s, 0), 1.0)
            fix_stress(s, up_face, 4, layers(up_rows, s, 1), 1.0)

        @pl.when(low_y_in)
        def _(s=s, copy=low_y_copy):
            copy.wait_recv()
            fix_stress(s, left_face, 1, layers(low_cols, s), -1.0)

        @pl.when(up_y_in)
        def _(s=s, copy=up_y_copy):
            copy.wait_recv()
            fix_stress(s, right_face, 3, layers(up_cols, s, 0), 1.0)
            fix_stress(s, right_face, 5, layers(up_cols, s, 1), 1.0)

    def term_row(x, carry):
        trace_sum, shear_sum = None, None
        for s in range(shots):
            e = [strain0[s, c, x] for c in range(6)]
            a = [st[s, 2, c, x] for c in range(6)]
            trace = (e[0] + e[1] + e[2]) * (a[0] + a[1] + a[2])
            product = (
                2.0 * (e[0] * a[0] + e[1] * a[1] + e[2] * a[2])
                + e[3] * a[3]
                + e[4] * a[4]
                + e[5] * a[5]
            )
            trace_sum = trace if s == 0 else trace_sum + trace
            shear_sum = product if s == 0 else shear_sum + product
        terms[0, x] = trace_sum
        terms[1, x] = shear_sum
        return carry

    shares = []
    for k in range(1, groups):
        peer = lax.rem(me + k, groups)
        lax.fori_loop(0, own, lambda i, carry, peer=peer: term_row(peer * own + i, carry), 0, unroll=2)
        copy = pltpu.make_async_remote_copy(
            src_ref=terms.at[:, pl.ds(peer * own, own)],
            dst_ref=landed.at[k - 1],
            send_sem=share_send_sem.at[k - 1],
            recv_sem=share_recv_sem.at[k - 1],
            device_id={"shot": peer},
            device_id_type=MESH,
        )
        copy.start()
        shares.append(copy)
    lax.fori_loop(0, own, lambda i, carry: term_row(me * own + i, carry), 0, unroll=2)
    for copy in shares:
        copy.wait_recv()
    total = terms[:, pl.ds(me * own, own)]
    for k in range(1, groups):
        total = total + landed[k - 1]
    kernels[...] = total * (1.0 / total_shots)
    for s in range(shots):
        sent(stress_faces[s])
        sent(motion_faces[s])
    for copy in shares:
        copy.wait_send()


def write_kernel(st, mo, kernels_in, new_velocity, new_stress, kernels, sems):
    shots = st.shape[0]
    copies = [pltpu.make_async_copy(kernels_in, kernels, sems.at[2 * shots])]
    for s in range(shots):
        copies.append(
            pltpu.make_async_copy(st.at[s, pl.ds(1, 2)], new_stress.at[s], sems.at[2 * s])
        )
        copies.append(
            pltpu.make_async_copy(mo.at[s, pl.ds(1, 2)], new_velocity.at[s], sems.at[2 * s + 1])
        )
    for copy in copies:
        copy.start()
    for copy in copies:
        copy.wait()


def shards(
    stress_fields,
    velocity_fields,
    lame,
    shear,
    density,
    lame_change,
    shear_change,
    density_change,
    source_cell,
    source_amp,
    receiver_cell,
):
    rows, cols, depth = lame.shape
    shots, waves = stress_fields.shape[:2]
    groups = lax.axis_size("shot")
    own = rows // groups
    every_column = cols * lax.axis_size("gy")
    f32 = jnp.float32
    hbm = pl.BlockSpec(memory_space=pltpu.HBM)
    smem = pl.BlockSpec(memory_space=pltpu.SMEM)
    vmem = pl.BlockSpec(memory_space=pltpu.VMEM)
    face_rows = [(shots, waves, cols, depth), (shots, waves, 2, cols, depth)]
    face_cols = [(shots, waves, rows, depth), (shots, waves, 2, rows, depth)]
    scratch = [
        (6, rows, cols, depth),
        None,
        (shots, rows, cols, depth),
        (shots, 3, rows, cols, depth),
        (shots, 6, rows, cols, depth),
        (3, rows, cols, depth),
        face_rows[0],
        face_rows[1],
        face_cols[0],
        face_cols[1],
        face_cols[0],
        face_cols[1],
        face_rows[1],
        face_rows[0],
        face_cols[1],
        face_cols[0],
        face_cols[1],
        face_cols[0],
        (max(groups - 1, 1), 3, own, cols, depth),
    ]
    scratch = [
        pltpu.VMEM(receiver_cell.shape, jnp.int32) if dims is None else pltpu.VMEM(dims, f32)
        for dims in scratch
    ]
    st, mo, kernels = pl.pallas_call(
        functools.partial(step_kernel, every_column, shots * groups),
        name="step",
        out_shape=(
            pltpu.VMEM((shots, waves, 6, rows, cols, depth), f32),
            pltpu.VMEM((shots, waves, 3, rows, cols, depth), f32),
            pltpu.VMEM((3, own, cols, depth), f32),
        ),
        in_specs=[hbm] * 9 + [smem] * 2,
        out_specs=(vmem, vmem, vmem),
        scratch_shapes=scratch
        + [
            pltpu.SemaphoreType.DMA((shots, 2)),
            pltpu.SemaphoreType.DMA((7,)),
            pltpu.SemaphoreType.DMA((8 * shots,)),
            pltpu.SemaphoreType.DMA((8 * shots,)),
            pltpu.SemaphoreType.DMA((max(groups - 1, 1),)),
            pltpu.SemaphoreType.DMA((max(groups - 1, 1),)),
        ],
        compiler_params=pltpu.CompilerParams(
            collective_id=0, has_side_effects=True, vmem_limit_bytes=VMEM_LIMIT
        ),
    )(
        *(
            pltpu.with_memory_space_constraint(array, pltpu.HBM)
            for array in (
                stress_fields,
                velocity_fields,
                lame,
                shear,
                density,
                lame_change,
                shear_change,
                density_change,
                receiver_cell,
                source_cell,
                source_amp,
            )
        ),
    )
    shape = lambda *dims: jax.ShapeDtypeStruct(dims, f32)
    return pl.pallas_call(
        write_kernel,
        name="write",
        out_shape=(
            shape(shots, 2, 3, rows, cols, depth),
            shape(shots, 2, 6, rows, cols, depth),
            shape(3, own, cols, depth),
        ),
        in_specs=[vmem] * 3,
        out_specs=(hbm, hbm, hbm),
        scratch_shapes=[pltpu.SemaphoreType.DMA((2 * shots + 1,))],
        compiler_params=pltpu.CompilerParams(vmem_limit_bytes=VMEM_LIMIT),
    )(st, mo, kernels)


def solution(mesh):
    return jax.shard_map(
        shards,
        mesh=mesh,
        in_specs=(
            P("shot", None, None, "gx", "gy", None),
            P("shot", None, None, "gx", "gy", None),
            P("gx", "gy", None),
            P("gx", "gy", None),
            P("gx", "gy", None),
            P("gx", "gy", None),
            P("gx", "gy", None),
            P("gx", "gy", None),
            P("shot"),
            P("shot"),
            P("shot", None),
        ),
        out_specs=(
            P("shot", None, None, "gx", "gy", None),
            P("shot", None, None, "gx", "gy", None),
            P(None, ("gx", "shot"), "gy", None),
        ),
        check_vma=False,
    )
```

```python
import functools

import jax
import jax.numpy as jnp
from jax import lax
from jax.experimental import pallas as pl
from jax.experimental.pallas import tpu as pltpu
from jax.sharding import PartitionSpec as P

RDEPTH = 2
COURANT = 0.25
MESH = pl.DeviceIdType.MESH
VMEM_LIMIT = 32 * 1024 * 1024


def shifted_up(tile, halo, axis):
    length = tile.shape[axis]
    index = lax.broadcasted_iota(jnp.int32, tile.shape, axis)
    return jnp.where(index == length - 1, halo, pltpu.roll(tile, length - 1, axis))


def shifted_down(tile, halo, axis):
    index = lax.broadcasted_iota(jnp.int32, tile.shape, axis)
    return jnp.where(index == 0, halo, pltpu.roll(tile, 1, axis))


def step_kernel(
    every_column,
    total_shots,
    stress,
    velocity,
    lame_in,
    shear_in,
    density_in,
    lame_change_in,
    shear_change_in,
    density_change_in,
    receivers_in,
    source_cell,
    source_amp,
    st,
    mo,
    kernels,
    params,
    receivers,
    record,
    accel0,
    strain0,
    terms,
    st_up_rows,
    st_low_rows,
    st_up_cols,
    st_low_cols,
    st_up_cols_out,
    st_low_cols_out,
    up_rows,
    low_rows,
    up_cols,
    low_cols,
    up_cols_out,
    low_cols_out,
    landed,
    load_sem,
    param_sem,
    send_sem,
    recv_sem,
    share_send_sem,
    share_recv_sem,
):
    shots, waves, _, rows, cols, depth = stress.shape
    gx, gy = lax.axis_index("gx"), lax.axis_index("gy")
    nx, ny = lax.axis_size("gx"), lax.axis_size("gy")
    me, groups = lax.axis_index("shot"), lax.axis_size("shot")
    own = rows // groups
    has_low_x, has_up_x = gx > 0, gx < nx - 1
    has_low_y, has_up_y = gy > 0, gy < ny - 1
    sides = (
        (has_low_x, {"gx": gx - 1}),
        (has_up_x, {"gx": gx + 1}),
        (has_low_y, {"gy": gy - 1}),
        (has_up_y, {"gy": gy + 1}),
    )
    barrier = pltpu.get_barrier_semaphore()
    for present, device in sides:

        @pl.when(present)
        def _(device=device):
            pl.semaphore_signal(barrier, inc=1, device_id=device, device_id_type=MESH)

    for k in range(1, groups):
        peer = lax.rem(me + k, groups)
        pl.semaphore_signal(barrier, inc=1, device_id={"shot": peer}, device_id_type=MESH)

    stress_loads = [
        pltpu.make_async_copy(stress.at[s], st.at[s], load_sem.at[s, 0]) for s in range(shots)
    ]
    motion_loads = [
        pltpu.make_async_copy(velocity.at[s], mo.at[s], load_sem.at[s, 1]) for s in range(shots)
    ]
    receiver_load = pltpu.make_async_copy(receivers_in, receivers, param_sem.at[6])
    sources = (density_in, density_change_in, lame_in, shear_in, lame_change_in, shear_change_in)
    param_loads = [
        pltpu.make_async_copy(source, params.at[i], param_sem.at[i])
        for i, source in enumerate(sources)
    ]
    stress_loads[0].start()
    receiver_load.start()
    for copy in stress_loads[1:] + param_loads[:2] + motion_loads + param_loads[2:]:
        copy.start()
    density, density_change, lame, shear, lame_change, shear_change = (
        params.at[i] for i in range(6)
    )

    def face(src, dst, slot, device):
        return pltpu.make_async_remote_copy(
            src_ref=src,
            dst_ref=dst,
            send_sem=send_sem.at[slot],
            recv_sem=recv_sem.at[slot],
            device_id=device,
            device_id_type=MESH,
        )

    low_x, up_x, low_y, up_y = (device for _, device in sides)
    stress_faces, motion_faces = [], []
    for s in range(shots):
        slot = 8 * s
        stress_faces.append(
            (
                (face(stress.at[s, :, 0, 0], st_up_rows.at[s], slot, low_x), has_low_x, has_up_x),
                (
                    face(stress.at[s, :, pl.ds(3, 2), rows - 1], st_low_rows.at[s], slot + 1, up_x),
                    has_up_x,
                    has_low_x,
                ),
                (face(st_up_cols_out.at[s], st_up_cols.at[s], slot + 2, low_y), has_low_y, has_up_y),
                (
                    face(st_low_cols_out.at[s], st_low_cols.at[s], slot + 3, up_y),
                    has_up_y,
                    has_low_y,
                ),
            )
        )
        motion_faces.append(
            (
                (
                    face(mo.at[s, :, pl.ds(1, 2), 0], up_rows.at[s], slot + 4, low_x),
                    has_low_x,
                    has_up_x,
                ),
                (face(mo.at[s, :, 0, rows - 1], low_rows.at[s], slot + 5, up_x), has_up_x, has_low_x),
                (face(up_cols_out.at[s], up_cols.at[s], slot + 6, low_y), has_low_y, has_up_y),
                (face(low_cols_out.at[s], low_cols.at[s], slot + 7, up_y), has_up_y, has_low_y),
            )
        )

    def send(faces):
        for copy, sends, _ in faces:

            @pl.when(sends)
            def _(copy=copy):
                copy.start()

    def sent(faces):
        for copy, sends, _ in faces:

            @pl.when(sends)
            def _(copy=copy):
                copy.wait_send()

    neighbours = groups - 1
    for present, _ in sides:
        neighbours = neighbours + present.astype(jnp.int32)
    pl.semaphore_wait(barrier, neighbours)
    for s in range(shots):
        send(stress_faces[s][:2])
    row_start, col_start = gx * rows, gy * cols

    for s in range(shots):
        stress_loads[s].wait()
        for w in range(waves):
            st_up_cols_out[s, w] = st[s, w, 1, :, 0, :]
            st_low_cols_out[s, w, 0] = st[s, w, 3, :, cols - 1, :]
            st_low_cols_out[s, w, 1] = st[s, w, 5, :, cols - 1, :]
        send(stress_faces[s][2:])

    receiver_load.wait()
    count = receivers.shape[1]
    plane = (lax.broadcasted_iota(jnp.int32, (count, depth), 1) == RDEPTH).astype(jnp.bfloat16)
    cell = (
        lax.broadcasted_iota(jnp.int32, (rows, cols, count), 0) + row_start
    ) * every_column + (lax.broadcasted_iota(jnp.int32, (rows, cols, count), 1) + col_start)
    cell = cell.reshape(rows * cols, count)
    for s in range(shots):
        marks = jnp.where(receivers[pl.ds(s, 1), :] == cell, 1.0, 0.0).astype(jnp.bfloat16)
        field = jnp.dot(marks, plane, preferred_element_type=jnp.float32)
        record[s] = field.reshape(rows, cols, depth)

    place = (
        lax.broadcasted_iota(jnp.int32, (cols, depth), 0) + col_start
    ) * depth + lax.broadcasted_iota(jnp.int32, (cols, depth), 1)
    param_loads[0].wait()
    param_loads[1].wait()

    for s in range(shots):
        motion_loads[s].wait()
        target, amplitude = source_cell[s], source_amp[s]

        def motion_row(x, carry, s=s, target=target, amplitude=amplitude):
            after = lax.rem(x + 1, rows)
            before = lax.rem(x + rows - 1, rows)
            last, first = x == rows - 1, x == 0
            buoyancy = 1.0 / density[x]
            scaled = COURANT * buoyancy
            change = density_change[x] * buoyancy
            accel = []
            for w in range(waves):
                sxx, syy, szz = st[s, w, 0, x], st[s, w, 1, x], st[s, w, 2, x]
                sxy, sxz, syz = st[s, w, 3, x], st[s, w, 4, x], st[s, w, 5, x]
                sxx_after = jnp.where(last, 0.0, st[s, w, 0, after])
                sxy_before = jnp.where(first, 0.0, st[s, w, 3, before])
                sxz_before = jnp.where(first, 0.0, st[s, w, 4, before])
                accel.append(
                    (
                        (sxx_after - sxx)
                        + (sxy - shifted_down(sxy, 0.0, 0))
                        + (sxz - shifted_down(sxz, 0.0, 1)),
                        (sxy - sxy_before)
                        + (shifted_up(syy, 0.0, 0) - syy)
                        + (syz - shifted_down(syz, 0.0, 1)),
                        (sxz - sxz_before)
                        + (syz - shifted_down(syz, 0.0, 0))
                        + (shifted_up(szz, 0.0, 1) - szz),
                    )
                )
            here = place + (x + row_start) * (every_column * depth)
            source = jnp.where(here == target, amplitude, 0.0)
            for c in range(3):
                first_wave = mo[s, 0, c, x] + scaled * accel[0][c]
                born = mo[s, 1, c, x] + scaled * (accel[1][c] - change * accel[0][c])
                adjoint = mo[s, 2, c, x] + scaled * accel[2][c]
                if c == 2:
                    first_wave = first_wave + scaled * source
                    adjoint = adjoint + scaled * record[s, x] * born
                accel0[s, c, x] = accel[0][c]
                mo[s, 0, c, x] = first_wave
                mo[s, 1, c, x] = born
                mo[s, 2, c, x] = adjoint
            return carry

        lax.fori_loop(0, rows, motion_row, 0, unroll=2)

    every = slice(None)
    low_face, up_face = (0, every), (rows - 1, every)
    left_face, right_face = (every, 0), (every, cols - 1)

    def fix_motion(s, where, c, halo, sign):
        at = where + (every,)
        buoyancy = 1.0 / density[at]
        scaled = COURANT * buoyancy
        change = density_change[at] * buoyancy
        d0, d1, d2 = (sign * halo[w] for w in range(waves))
        accel0[(s, c) + at] += d0
        mo[(s, 0, c) + at] += scaled * d0
        born = scaled * (d1 - change * d0)
        mo[(s, 1, c) + at] += born
        adjoint = scaled * d2
        if c == 2:
            adjoint = adjoint + scaled * record[(s,) + at] * born
        mo[(s, 2, c) + at] += adjoint

    def layers(ref, s, which=None):
        if which is None:
            return [ref[s, w] for w in range(waves)]
        return [ref[s, w, which] for w in range(waves)]

    for s in range(shots):
        (up_x_copy, _, up_x_in), (low_x_copy, _, low_x_in), (up_y_copy, _, up_y_in), (
            low_y_copy,
            _,
            low_y_in,
        ) = stress_faces[s]

        @pl.when(up_y_in)
        def _(s=s, copy=up_y_copy):
            copy.wait_recv()
            fix_motion(s, right_face, 1, layers(st_up_cols, s), 1.0)

        @pl.when(low_y_in)
        def _(s=s, copy=low_y_copy):
            copy.wait_recv()
            fix_motion(s, left_face, 0, layers(st_low_cols, s, 0), -1.0)
            fix_motion(s, left_face, 2, layers(st_low_cols, s, 1), -1.0)

        @pl.when(up_x_in)
        def _(s=s, copy=up_x_copy):
            copy.wait_recv()
            fix_motion(s, up_face, 0, layers(st_up_rows, s), 1.0)

        send(motion_faces[s][1:2])

        @pl.when(low_x_in)
        def _(s=s, copy=low_x_copy):
            copy.wait_recv()
            fix_motion(s, low_face, 1, layers(st_low_rows, s, 0), -1.0)
            fix_motion(s, low_face, 2, layers(st_low_rows, s, 1), -1.0)

        send(motion_faces[s][:1])
        for w in range(waves):
            up_cols_out[s, w, 0] = mo[s, w, 0, :, 0, :]
            up_cols_out[s, w, 1] = mo[s, w, 2, :, 0, :]
            low_cols_out[s, w] = mo[s, w, 1, :, cols - 1, :]
        send(motion_faces[s][2:])

    for copy in param_loads[2:]:
        copy.wait()

    def modulus(strain, first, second, twice):
        trace = first * (strain[0] + strain[1] + strain[2])
        return [trace + twice * strain[i] for i in range(3)] + [
            second * strain[i] for i in range(3, 6)
        ]

    for s in range(shots):

        def stress_row(x, carry, s=s):
            after = lax.rem(x + 1, rows)
            before = lax.rem(x + rows - 1, rows)
            last, first = x == rows - 1, x == 0
            strain, adjoint_motion = [], None
            for w in range(waves):
                vx, vy, vz = mo[s, w, 0, x], mo[s, w, 1, x], mo[s, w, 2, x]
                adjoint_motion = (vx, vy, vz)
                vx_before = jnp.where(first, 0.0, mo[s, w, 0, before])
                vy_after = jnp.where(last, 0.0, mo[s, w, 1, after])
                vz_after = jnp.where(last, 0.0, mo[s, w, 2, after])
                strain.append(
                    (
                        vx - vx_before,
                        vy - shifted_down(vy, 0.0, 0),
                        vz - shifted_down(vz, 0.0, 1),
                        (shifted_up(vx, 0.0, 0) - vx) + (vy_after - vy),
                        (shifted_up(vx, 0.0, 1) - vx) + (vz_after - vz),
                        (shifted_up(vy, 0.0, 1) - vy) + (shifted_up(vz, 0.0, 0) - vz),
                    )
                )
            first_modulus, second_modulus = lame[x], shear[x]
            twice = 2.0 * second_modulus
            second_change = shear_change[x]
            born = modulus(strain[1], first_modulus, second_modulus, twice)
            changed = modulus(strain[0], lame_change[x], second_change, 2.0 * second_change)
            adjoint = modulus(strain[2], first_modulus, second_modulus, twice)
            for c in range(6):
                strain0[s, c, x] = strain[0][c]
                st[s, 1, c, x] = st[s, 1, c, x] + COURANT * (born[c] + changed[c])
                st[s, 2, c, x] = st[s, 2, c, x] + COURANT * adjoint[c]
            total = (
                accel0[s, 0, x] * adjoint_motion[0]
                + accel0[s, 1, x] * adjoint_motion[1]
                + accel0[s, 2, x] * adjoint_motion[2]
            )
            total = (1.0 / density[x]) * total
            terms[2, x] = total if s == 0 else terms[2, x] + total
            return carry

        lax.fori_loop(0, rows, stress_row, 0, unroll=2)

    def fix_stress(s, where, c, halo, sign):
        at = where + (every,)
        d0, d1, d2 = (sign * halo[w] for w in range(waves))
        strain0[(s, c) + at] += d0
        second = shear[at]
        own_born = second * d1 + shear_change[at] * d0
        own_adjoint = second * d2
        if c >= 3:
            st[(s, 1, c) + at] += COURANT * own_born
            st[(s, 2, c) + at] += COURANT * own_adjoint
            return
        born = lame[at] * d1 + lame_change[at] * d0
        adjoint = lame[at] * d2
        for i in range(3):
            more_born, more_adjoint = born, adjoint
            if i == c:
                more_born, more_adjoint = born + 2.0 * own_born, adjoint + 2.0 * own_adjoint
            st[(s, 1, i) + at] += COURANT * more_born
            st[(s, 2, i) + at] += COURANT * more_adjoint

    for s in range(shots):
        (up_x_copy, _, up_x_in), (low_x_copy, _, low_x_in), (up_y_copy, _, up_y_in), (
            low_y_copy,
            _,
            low_y_in,
        ) = motion_faces[s]

        @pl.when(low_x_in)
        def _(s=s, copy=low_x_copy):
            copy.wait_recv()
            fix_stress(s, low_face, 0, layers(low_rows, s), -1.0)

        @pl.when(up_x_in)
        def _(s=s, copy=up_x_copy):
            copy.wait_recv()
            fix_stress(s, up_face, 3, layers(up_rows, s, 0), 1.0)
            fix_stress(s, up_face, 4, layers(up_rows, s, 1), 1.0)

        @pl.when(low_y_in)
        def _(s=s, copy=low_y_copy):
            copy.wait_recv()
            fix_stress(s, left_face, 1, layers(low_cols, s), -1.0)

        @pl.when(up_y_in)
        def _(s=s, copy=up_y_copy):
            copy.wait_recv()
            fix_stress(s, right_face, 3, layers(up_cols, s, 0), 1.0)
            fix_stress(s, right_face, 5, layers(up_cols, s, 1), 1.0)

    def term_row(x, carry):
        trace_sum, shear_sum = None, None
        for s in range(shots):
            e = [strain0[s, c, x] for c in range(6)]
            a = [st[s, 2, c, x] for c in range(6)]
            trace = (e[0] + e[1] + e[2]) * (a[0] + a[1] + a[2])
            product = (
                2.0 * (e[0] * a[0] + e[1] * a[1] + e[2] * a[2])
                + e[3] * a[3]
                + e[4] * a[4]
                + e[5] * a[5]
            )
            trace_sum = trace if s == 0 else trace_sum + trace
            shear_sum = product if s == 0 else shear_sum + product
        terms[0, x] = trace_sum
        terms[1, x] = shear_sum
        return carry

    shares = []
    for k in range(1, groups):
        peer = lax.rem(me + k, groups)
        lax.fori_loop(0, own, lambda i, carry, peer=peer: term_row(peer * own + i, carry), 0, unroll=2)
        copy = pltpu.make_async_remote_copy(
            src_ref=terms.at[:, pl.ds(peer * own, own)],
            dst_ref=landed.at[k - 1],
            send_sem=share_send_sem.at[k - 1],
            recv_sem=share_recv_sem.at[k - 1],
            device_id={"shot": peer},
            device_id_type=MESH,
        )
        copy.start()
        shares.append(copy)
    lax.fori_loop(0, own, lambda i, carry: term_row(me * own + i, carry), 0, unroll=2)
    for copy in shares:
        copy.wait_recv()
    total = terms[:, pl.ds(me * own, own)]
    for k in range(1, groups):
        total = total + landed[k - 1]
    kernels[...] = total * (1.0 / total_shots)
    for s in range(shots):
        sent(stress_faces[s])
        sent(motion_faces[s])
    for copy in shares:
        copy.wait_send()


def write_kernel(st, mo, kernels_in, new_velocity, new_stress, kernels, sems):
    shots = st.shape[0]
    copies = [pltpu.make_async_copy(kernels_in, kernels, sems.at[2 * shots])]
    for s in range(shots):
        copies.append(
            pltpu.make_async_copy(st.at[s, pl.ds(1, 2)], new_stress.at[s], sems.at[2 * s])
        )
        copies.append(
            pltpu.make_async_copy(mo.at[s, pl.ds(1, 2)], new_velocity.at[s], sems.at[2 * s + 1])
        )
    for copy in copies:
        copy.start()
    for copy in copies:
        copy.wait()


def shards(
    stress_fields,
    velocity_fields,
    lame,
    shear,
    density,
    lame_change,
    shear_change,
    density_change,
    source_cell,
    source_amp,
    receiver_cell,
):
    rows, cols, depth = lame.shape
    shots, waves = stress_fields.shape[:2]
    groups = lax.axis_size("shot")
    own = rows // groups
    every_column = cols * lax.axis_size("gy")
    f32 = jnp.float32
    hbm = pl.BlockSpec(memory_space=pltpu.HBM)
    smem = pl.BlockSpec(memory_space=pltpu.SMEM)
    vmem = pl.BlockSpec(memory_space=pltpu.VMEM)
    face_rows = [(shots, waves, cols, depth), (shots, waves, 2, cols, depth)]
    face_cols = [(shots, waves, rows, depth), (shots, waves, 2, rows, depth)]
    scratch = [
        (6, rows, cols, depth),
        None,
        (shots, rows, cols, depth),
        (shots, 3, rows, cols, depth),
        (shots, 6, rows, cols, depth),
        (3, rows, cols, depth),
        face_rows[0],
        face_rows[1],
        face_cols[0],
        face_cols[1],
        face_cols[0],
        face_cols[1],
        face_rows[1],
        face_rows[0],
        face_cols[1],
        face_cols[0],
        face_cols[1],
        face_cols[0],
        (max(groups - 1, 1), 3, own, cols, depth),
    ]
    scratch = [
        pltpu.VMEM(receiver_cell.shape, jnp.int32) if dims is None else pltpu.VMEM(dims, f32)
        for dims in scratch
    ]
    st, mo, kernels = pl.pallas_call(
        functools.partial(step_kernel, every_column, shots * groups),
        name="step",
        out_shape=(
            pltpu.VMEM((shots, waves, 6, rows, cols, depth), f32),
            pltpu.VMEM((shots, waves, 3, rows, cols, depth), f32),
            pltpu.VMEM((3, own, cols, depth), f32),
        ),
        in_specs=[hbm] * 9 + [smem] * 2,
        out_specs=(vmem, vmem, vmem),
        scratch_shapes=scratch
        + [
            pltpu.SemaphoreType.DMA((shots, 2)),
            pltpu.SemaphoreType.DMA((7,)),
            pltpu.SemaphoreType.DMA((8 * shots,)),
            pltpu.SemaphoreType.DMA((8 * shots,)),
            pltpu.SemaphoreType.DMA((max(groups - 1, 1),)),
            pltpu.SemaphoreType.DMA((max(groups - 1, 1),)),
        ],
        compiler_params=pltpu.CompilerParams(
            collective_id=0, has_side_effects=True, vmem_limit_bytes=VMEM_LIMIT
        ),
    )(
        *(
            pltpu.with_memory_space_constraint(array, pltpu.HBM)
            for array in (
                stress_fields,
                velocity_fields,
                lame,
                shear,
                density,
                lame_change,
                shear_change,
                density_change,
                receiver_cell,
                source_cell,
                source_amp,
            )
        ),
    )
    shape = lambda *dims: jax.ShapeDtypeStruct(dims, f32)
    return pl.pallas_call(
        write_kernel,
        name="write",
        out_shape=(
            shape(shots, 2, 3, rows, cols, depth),
            shape(shots, 2, 6, rows, cols, depth),
            shape(3, own, cols, depth),
        ),
        in_specs=[vmem] * 3,
        out_specs=(hbm, hbm, hbm),
        scratch_shapes=[pltpu.SemaphoreType.DMA((2 * shots + 1,))],
        compiler_params=pltpu.CompilerParams(vmem_limit_bytes=VMEM_LIMIT),
    )(st, mo, kernels)


def solution(mesh):
    return jax.shard_map(
        shards,
        mesh=mesh,
        in_specs=(
            P("shot", None, None, "gx", "gy", None),
            P("shot", None, None, "gx", "gy", None),
            P("gx", "gy", None),
            P("gx", "gy", None),
            P("gx", "gy", None),
            P("gx", "gy", None),
            P("gx", "gy", None),
            P("gx", "gy", None),
            P("shot"),
            P("shot"),
            P("shot", None),
        ),
        out_specs=(
            P("shot", None, None, "gx", "gy", None),
            P("shot", None, None, "gx", "gy", None),
            P(None, ("gx", "shot"), "gy", None),
        ),
        check_vma=False,
    )
```
